256 devices in a mesh: ctx: 32 (over z, x), head: 8 (over y, core).
Axes of the slice: x: 4, y: 4, z: 8, core: 2. Of those that a mesh axis runs over, the one named last changes fastest.
Arguments:
- layer_input: bfloat16 [65536, 3072], P(('ctx', 'head')), may hold values from -1.1953125 to 1.1953125
- cotangent: bfloat16 [65536, 3072], P(('ctx', 'head')), may hold values from -1.1953125 to 1.1953125
- b_proj: bfloat16 [65536, 128], P('ctx'), may hold values from -0.1796875 to 0.1796875
- c_proj: bfloat16 [65536, 128], P('ctx'), may hold values from -0.1796875 to 0.1796875
- log_decay: float32 [65536, 48], P('ctx', 'head'), may hold values from -1 to 0
- resets: int32 [65536], P('ctx'), may hold values from 0 to 1, as said below
- agent_ids: int32 [65536], P('ctx'), may hold values from 0 to 63
- skip_gain: float32 [48], replicated, may hold values from 0.25 to 2.5
- agent_table: bfloat16 [64, 3072], P(None, 'head'), may hold values from -0.59765625 to 0.59765625
Outputs:
- layer_output: bfloat16 [65536, 3072], P(('ctx', 'head'))
- input_grad: bfloat16 [65536, 3072], P(('ctx', 'head'))
- b_grad: bfloat16 [65536, 128], P(('ctx', 'head'))
- c_grad: bfloat16 [65536, 128], P(('ctx', 'head'))
The draws below stay inside these ranges and needn't reach their ends.
Inputs may be any that keep to these rules, and one draw needn't show every extreme that they name: `resets`: exactly 4 ones, one in each of 4 equal stretches of the sequence and never at a stretch's first token.
All inputs are finite; a program needn't handle non-finite values.
Results may differ from the reference program's by a relative error of at most 0.0085.
Values may be sent and summed in bfloat16 or wider, within the bound.
A program may use at most 256 MiB of HBM per device.

```python
import jax
import jax.numpy as jnp
from jax import lax

HEAD_TOTAL = 48
HEAD_DIM = 64
STATE = 128
TRACT = 256
AGENTS = 64
RESETS = 4
TRACTS_DEV = 8
TOKEN_TOTAL = 65536


def draw_log_decay(key, part):
    random_keys_split = jax.random.split(key, 6)
    device_span = TRACTS_DEV * TRACT
    regions = TOKEN_TOTAL // device_span
    fast_share = 0.3
    middle_share = 0.2
    category = jax.random.uniform(random_keys_split[0], (HEAD_TOTAL,))
    spread = jax.random.uniform(random_keys_split[1], (HEAD_TOTAL,))
    fast_rate = jnp.exp(jnp.log(1.0 / 50.0) + spread * jnp.log(50.0 / 30.0))
    middle = jnp.exp(jnp.log(0.5 / device_span) + spread * jnp.log(8.0))
    slow_rate = jnp.exp(jnp.log(0.02 / TOKEN_TOTAL) + spread * jnp.log(15.0))
    head_rate = jnp.where(category < fast_share, fast_rate, jnp.where(category < fast_share + middle_share, middle, slow_rate))
    token_factor = jax.random.uniform(random_keys_split[2], (TOKEN_TOTAL, HEAD_TOTAL), minval=0.5, maxval=1.5)
    region = jnp.exp(jax.random.uniform(random_keys_split[3], (regions, 1, HEAD_TOTAL), minval=-0.5, maxval=0.5))
    region = jnp.broadcast_to(region, (regions, device_span, HEAD_TOTAL)).reshape(TOKEN_TOTAL, HEAD_TOTAL)
    spike_position = jax.random.randint(random_keys_split[4], (2,), 0, TOKEN_TOTAL)
    reset_hit = jnp.any(jnp.arange(TOKEN_TOTAL, dtype=jnp.int32)[:, None] == spike_position[None, :], axis=1)
    spike_objective = jax.random.uniform(random_keys_split[5], (HEAD_TOTAL,), minval=0.22, maxval=0.69)
    stable_decay = head_rate[None, :] * token_factor * region
    return (-stable_decay - jnp.where(reset_hit[:, None], spike_objective[None, :], 0.0)).astype(jnp.float32)


def draw_resets(key, part):
    stretch = TOKEN_TOTAL // RESETS
    offsets = jax.random.randint(key, (RESETS,), 1, stretch)
    places = jnp.arange(RESETS, dtype=jnp.int32) * stretch + offsets
    marked = jnp.any(jnp.arange(TOKEN_TOTAL, dtype=jnp.int32)[:, None] == places[None, :], axis=1)
    return marked.astype(jnp.int32)


def plant(values, key, low, largest):
    dims = values.shape
    index_at = [jax.random.randint(jax.random.fold_in(key, axis), (), 0, dims[axis]) for axis in range(len(dims))]
    values = values.at[tuple(index_at)].set(low)
    longest = dims.index(max(dims))
    index_at[longest] = (index_at[longest] + 1) % dims[longest]
    return values.at[tuple(index_at)].set(largest)


def block_scale(key, shape, cuts, least, top_value):
    level, own = 1.0, jax.random.fold_in(key, 6)
    for position, parts in cuts:
        draws = jnp.exp(jax.random.uniform(jax.random.fold_in(own, position), (parts,), jnp.float32, least / len(cuts), top_value / len(cuts)))
        level = level * jnp.repeat(draws, shape[position] // parts).reshape([-1 if axis == position else 1 for axis in range(len(shape))])
    return level


def gaussian(stream_key, dims, width, limit, cuts=(), kind=jnp.bfloat16):
    entries = jax.random.normal(stream_key, dims, jnp.float32) * width
    if len(cuts) > 0:
        entries = block_scale(stream_key, dims, cuts, -0.22, 0.18) * entries
    return jnp.clip(entries, min=-limit, max=limit).astype(kind)


def setup_inputs(seed: int = 0) -> dict:
    streams_of = jax.random.split(jax.random.key(seed), 10)
    return {
        "layer_input": gaussian(streams_of[0], (TOKEN_TOTAL, HEAD_TOTAL * HEAD_DIM), 0.2, 1.1953125, ((0, 256),)),
        "cotangent": gaussian(streams_of[1], (TOKEN_TOTAL, HEAD_TOTAL * HEAD_DIM), 0.2, 1.1953125, ((0, 256),)),
        "b_proj": gaussian(streams_of[2], (TOKEN_TOTAL, STATE), 0.03, 0.1796875, ((0, 32),)),
        "c_proj": gaussian(streams_of[3], (TOKEN_TOTAL, STATE), 0.03, 0.1796875, ((0, 32),)),
        "log_decay": draw_log_decay(jax.random.fold_in(streams_of[9], 71), 0),
        "resets": draw_resets(jax.random.fold_in(streams_of[9], 71), 0),
        "agent_ids": plant(jax.random.randint(streams_of[6], (TOKEN_TOTAL,), 0, AGENTS), jax.random.fold_in(streams_of[6], 1), 0, AGENTS - 1).astype(jnp.int32),
        "skip_gain": jnp.clip(jax.random.uniform(streams_of[7], (HEAD_TOTAL,), jnp.float32, 0.25, 2.5), 0.25, 2.5),
        "agent_table": gaussian(streams_of[8], (AGENTS, HEAD_TOTAL * HEAD_DIM), 0.1, 0.59765625, ((1, 8),)),
    }


def tract_summary(inputs, grads, b_rows, c_rows, log_decay, resets):
    exact = lax.Precision.HIGHEST
    log_run = jnp.cumsum(log_decay, axis=0)
    resets_seen = jnp.cumsum(resets, axis=0, dtype=jnp.int32)
    log_end = log_run[-1]
    start_weight = jnp.where((resets_seen == 0)[:, None], jnp.exp(log_run), 0.0)
    end_weight = jnp.where((resets_seen == resets_seen[-1])[:, None], jnp.exp(log_end[None, :] - log_run), 0.0)
    tract_decay = jnp.where(resets_seen[-1] == 0, jnp.exp(log_end), 0.0)
    inputs_end = (end_weight[:, :, None] * inputs.astype(jnp.float32)).astype(jnp.bfloat16)
    grads_start = (start_weight[:, :, None] * grads.astype(jnp.float32)).astype(jnp.bfloat16)
    tract_state = jnp.einsum("thp,tn->hpn", inputs_end.astype(jnp.float32), b_rows.astype(jnp.float32), precision=exact)
    tract_adjoint = jnp.einsum("thp,tn->hpn", grads_start.astype(jnp.float32), c_rows.astype(jnp.float32), precision=exact)
    weights = (start_weight, end_weight, inputs_end, grads_start)
    return log_run, resets_seen, weights, (tract_decay, tract_state, tract_adjoint)


def tract_intra(inputs, grads, b_rows, c_rows, log_run, resets_seen):
    exact = lax.Precision.HIGHEST
    length = log_run.shape[0]
    row_index = lax.broadcasted_iota(jnp.int32, (length, length), 0)
    col_index = lax.broadcasted_iota(jnp.int32, (length, length), 1)
    visible = (col_index <= row_index) & (resets_seen[:, None] == resets_seen[None, :])
    per_head = log_run.T
    log_gap = per_head[:, :, None] - per_head[:, None, :]
    decay_mask = jnp.where(visible[None], jnp.exp(jnp.minimum(log_gap, 0.0)), 0.0)
    c_dot_b = jnp.dot(c_rows, b_rows.T, preferred_element_type=jnp.float32)
    mixing = (decay_mask * c_dot_b[None]).astype(jnp.bfloat16).astype(jnp.float32)
    inputs_wide = inputs.astype(jnp.float32)
    grads_wide = grads.astype(jnp.float32)
    crossed = jnp.einsum("thp,shp->hts", grads_wide, inputs_wide, precision=exact)
    paired = (decay_mask * crossed).astype(jnp.bfloat16).astype(jnp.float32)
    y_local = jnp.einsum("hts,shp->thp", mixing, inputs_wide, precision=exact)
    du_local = jnp.einsum("hts,thp->shp", mixing, grads_wide, precision=exact)
    dc_local = jnp.einsum("hts,sn->tn", paired, b_rows.astype(jnp.float32), precision=exact)
    db_local = jnp.einsum("hts,tn->sn", paired, c_rows.astype(jnp.float32), precision=exact)
    return y_local, du_local, dc_local, db_local


def tract_carry(b_rows, c_rows, weights, state_in, adjoint_in):
    exact = lax.Precision.HIGHEST
    start_weight, end_weight, inputs_end, grads_start = weights
    y_carry = start_weight[:, :, None] * jnp.einsum("tn,hpn->thp", c_rows.astype(jnp.float32), state_in, precision=exact)
    du_carry = end_weight[:, :, None] * jnp.einsum("tn,hpn->thp", b_rows.astype(jnp.float32), adjoint_in, precision=exact)
    dc_carry = jnp.einsum("thp,hpn->tn", grads_start.astype(jnp.float32), state_in, precision=exact)
    db_carry = jnp.einsum("thp,hpn->tn", inputs_end.astype(jnp.float32), adjoint_in, precision=exact)
    return y_carry, du_carry, dc_carry, db_carry


def reference(layer_input, cotangent, b_proj, c_proj, log_decay, resets, agent_ids, skip_gain, agent_table):
    tract_count = TOKEN_TOTAL // TRACT
    feature_width = HEAD_TOTAL * HEAD_DIM
    state_zero = jnp.zeros((HEAD_TOTAL, HEAD_DIM, STATE), jnp.float32)

    def pieces(tract_index):
        first = (tract_index * TRACT).astype(jnp.int32)

        def slice_rows(values):
            return lax.dynamic_slice_in_dim(values, first, TRACT, 0)

        embedded = jnp.take(agent_table, slice_rows(agent_ids), axis=0)
        inputs = (slice_rows(layer_input).astype(jnp.float32) + embedded.astype(jnp.float32)).astype(jnp.bfloat16)
        inputs = inputs.reshape(TRACT, HEAD_TOTAL, HEAD_DIM)
        grads = slice_rows(cotangent).reshape(TRACT, HEAD_TOTAL, HEAD_DIM)
        return inputs, grads, slice_rows(b_proj), slice_rows(c_proj), slice_rows(log_decay), slice_rows(resets)

    def forward(state_in, tract_index):
        inputs, grads, b_rows, c_rows, decays, flags = pieces(tract_index)
        log_run, resets_seen, weights, summaries = tract_summary(inputs, grads, b_rows, c_rows, decays, flags)
        local = tract_intra(inputs, grads, b_rows, c_rows, log_run, resets_seen)
        carried = tract_carry(b_rows, c_rows, weights, state_in, state_zero)
        output = local[0] + carried[0] + skip_gain[None, :, None] * inputs.astype(jnp.float32)
        c_total = local[2] + carried[2]
        state_next = summaries[0][:, None, None] * state_in + summaries[1]
        return state_next, (output.astype(jnp.bfloat16).reshape(TRACT, feature_width), c_total.astype(jnp.bfloat16))

    def backward(adjoint_in, tract_index):
        inputs, grads, b_rows, c_rows, decays, flags = pieces(tract_index)
        log_run, resets_seen, weights, summaries = tract_summary(inputs, grads, b_rows, c_rows, decays, flags)
        local = tract_intra(inputs, grads, b_rows, c_rows, log_run, resets_seen)
        carried = tract_carry(b_rows, c_rows, weights, state_zero, adjoint_in)
        du_total = local[1] + carried[1] + skip_gain[None, :, None] * grads.astype(jnp.float32)
        b_total = local[3] + carried[3]
        adjoint_next = summaries[0][:, None, None] * adjoint_in + summaries[2]
        return adjoint_next, (du_total.astype(jnp.bfloat16).reshape(TRACT, feature_width), b_total.astype(jnp.bfloat16))

    order = jnp.arange(tract_count, dtype=jnp.int32)
    unused_state, forward_out = lax.scan(forward, state_zero, order)
    unused_adjoint, backward_out = lax.scan(backward, state_zero, order, reverse=True)
    layer_output = forward_out[0].reshape(TOKEN_TOTAL, feature_width)
    c_grad = forward_out[1].reshape(TOKEN_TOTAL, STATE)
    input_grad = backward_out[0].reshape(TOKEN_TOTAL, feature_width)
    b_grad = backward_out[1].reshape(TOKEN_TOTAL, STATE)
    return layer_output, input_grad, b_grad, c_grad
```

```python
import functools

import jax
import jax.numpy as jnp
from jax import lax
from jax.experimental import pallas as pl
from jax.experimental.pallas import tpu as pltpu
from jax.sharding import PartitionSpec as P

MESH = pl.DeviceIdType.MESH
F32 = jnp.float32
BF16 = jnp.bfloat16
TOK = 256
FEAT = 3072
STATE = 128
GROUP = 384
SLICE = 768
HALF = 64
PIECE = 16
CHUNKS = 2
LOG2E = 1.4426950408889634


def dot(a, b):
    return jnp.dot(a, b, preferred_element_type=F32)


def dot_nt(a, b):
    return lax.dot_general(a, b, (((1,), (1,)), ((), ())), preferred_element_type=F32)


def dot_tn(a, b):
    return lax.dot_general(a, b, (((0,), (0,)), ((), ())), preferred_element_type=F32)


def split3(a):
    hi = a.astype(BF16)
    rest = a - hi.astype(F32)
    mid = rest.astype(BF16)
    low = (rest - mid.astype(F32)).astype(BF16)
    return hi, mid, low


def kernel(
    x_hbm, g_hbm, b_hbm, c_hbm, ld_hbm, tab_hbm, resets_ref, ids_ref, skip_ref,
    out, proj_out,
    x, g, cb, cbt, ld, tab, logs, cbm, vis, paired, onehot, wcat, spread,
    u, gi, wts, loc, acc, sa, own_d, partner_sa, partner_d,
    tot, tot_d, yin, yin_d, ypre, gt, gd, xin, xin_d, xpre, rt, rd, zin, zin_d,
    xo, gc, yo, w, full,
    lsem, hs, hr, ps, pr, pds, pdr, y1s, y1r, yds, ydr, x1s, x1r, xds, xdr, z1s, z1r, zds, zdr,
    x2s, x2r, y2s, y2r, p2s, p2r, ready, ld_own,
):
    cx = lax.axis_index("ctx")
    hd = lax.axis_index("head")
    zz, xx = cx // 4, cx % 4
    yy, core = hd // 2, hd % 2
    mydir = 1 - core
    pos_y = core * yy + (1 - core) * (3 - yy)
    pos_x = core * xx + (1 - core) * (3 - xx)
    pos_z = core * zz + (1 - core) * (7 - zz)

    def at4(q):
        return core * q + (1 - core) * (3 - q)

    def at8(q):
        return core * q + (1 - core) * (7 - q)

    def remote(src, dst, s, r, dev):
        return pltpu.make_async_remote_copy(
            src_ref=src, dst_ref=dst, send_sem=s, recv_sem=r, device_id=dev, device_id_type=MESH
        )

    def half(i):
        return pl.ds(i * HALF, HALF)

    def piece(i, place):
        return pl.ds(pl.multiple_of(i * HALF + place * PIECE, PIECE), PIECE)

    ld[:, 6:8, :] = jnp.zeros((8, 2, TOK), F32)
    zin_d[...] = jnp.zeros_like(zin_d)
    zin[...] = jnp.zeros_like(zin)

    barrier = pltpu.get_barrier_semaphore()
    for k in (2, 6, 1, 7):
        pl.semaphore_signal(barrier, inc=1, device_id=(((zz + k) % 8) * 4 + xx, hd), device_id_type=MESH)
    for k in range(1, 8):
        pl.semaphore_signal(barrier, inc=1, device_id=(cx, (hd + k) % 8), device_id_type=MESH)
    for k in range(1, 4):
        pl.semaphore_signal(barrier, inc=1, device_id=(zz * 4 + (xx + k) % 4, hd), device_id_type=MESH)

    mine = pl.ds(pl.multiple_of(hd * TOK, TOK), TOK)
    own_ld = pltpu.make_async_copy(ld_hbm, ld_own, lsem.at[5])
    loads = [
        pltpu.make_async_copy(g_hbm, g, lsem.at[0]),
        pltpu.make_async_copy(b_hbm.at[mine, :], cb.at[1], lsem.at[1]),
        pltpu.make_async_copy(c_hbm.at[mine, :], cb.at[0], lsem.at[2]),
        pltpu.make_async_copy(x_hbm, x, lsem.at[3]),
    ]
    own_tab = pltpu.make_async_copy(tab_hbm, tab.at[hd], lsem.at[4])
    own_ld.start()
    own_tab.start()
    for one in (loads[1], loads[2], loads[0], loads[3]):
        one.start()

    paired[...] = jnp.zeros_like(paired)

    def build(j, carry):
        r3 = lax.broadcasted_iota(jnp.int32, (192, GROUP), 0)
        c3 = lax.broadcasted_iota(jnp.int32, (192, GROUP), 1)
        spread[:, pl.ds(pl.multiple_of(j * GROUP, 128), GROUP)] = (
            ((r3 & 63) == 8 * j + (c3 >> 6)).astype(F32).astype(BF16)
        )
        return carry

    lax.fori_loop(0, 8, build, 0)
    own_ld.wait()
    own_tab.wait()
    pl.semaphore_wait(barrier, 14)

    def ld_copy(k):
        to = (hd + k) % 8
        theirs = pl.ds(pl.multiple_of(to * TOK, TOK), TOK)
        return remote(
            ld_own.at[:, theirs], ld.at[hd, pl.ds(0, 6), :], hs.at[0, k - 1], hr.at[0, k - 1], (cx, to)
        )

    def tab_copy(k):
        return remote(tab.at[hd], tab.at[hd], hs.at[1, k - 1], hr.at[1, k - 1], (cx, (hd + k) % 8))

    for k in (4, 3, 5, 2, 6, 1, 7):
        ld_copy(k).start()
    for k in (4, 3, 5, 2, 6, 1, 7):
        tab_copy(k).start()
    for k in (2, 6):
        pl.semaphore_signal(ready, inc=1, device_id=(((zz + k) % 8) * 4 + xx, hd), device_id_type=MESH)
    ld[hd, 0:6, :] = ld_own[:, mine]

    row = lax.broadcasted_iota(jnp.int32, (TOK, TOK), 0)
    col = lax.broadcasted_iota(jnp.int32, (TOK, TOK), 1)
    upper = (row <= col).astype(F32).astype(BF16)
    flags = resets_ref[:, mine].astype(F32)
    seen = dot(jnp.broadcast_to(flags, (8, TOK)).astype(BF16), upper)
    seen_row = seen[0:1, :]
    seen_col = jnp.transpose(seen)[:, 0:1]
    visible = ((col <= row) & (seen_row == seen_col)).astype(F32)
    vis[...] = visible
    loads[1].wait()
    loads[2].wait()
    cbm[...] = dot_nt(cb[0], cb[1]) * visible
    cbt[0] = jnp.transpose(cb[0].astype(F32)).astype(BF16)
    cbt[1] = jnp.transpose(cb[1].astype(F32)).astype(BF16)
    agent = lax.broadcasted_iota(jnp.int32, (64, TOK), 0)
    picked = (agent == ids_ref[:, mine]).astype(F32)
    onehot[...] = jnp.transpose(picked).astype(BF16)

    for k in range(1, 8):
        ld_copy(k).wait_recv()
    hi, mid, low = split3(ld[...].reshape(64, TOK))
    run = (dot(hi, upper) + dot(mid, upper) + dot(low, upper)) * LOG2E
    logs[...] = run.reshape(8, 8, TOK)
    run_end = run[:, TOK - 1 : TOK]
    seen_end = seen_row[:, TOK - 1 : TOK]
    start = jnp.where(seen_row == 0, jnp.exp2(run), 0.0)
    end = jnp.where(seen_row == seen_end, jnp.exp2(jnp.minimum(run_end - run, 0.0)), 0.0)
    for index, value in ((0, start), (1, end)):
        turned = jnp.transpose(value)
        wcat[index] = jnp.concatenate(split3(turned), axis=1)

    loads[0].wait()

    def columns(j):
        return pl.ds(pl.multiple_of(j * GROUP, 128), GROUP)

    def prepare_adjoint(j, carry):
        cols = columns(j)
        weight = dot(wcat[0], spread[:, cols])
        own_d[:, cols] = weight[TOK - 1 : TOK, :]
        starts = (weight * g[:, cols].astype(F32)).astype(BF16)
        part = pl.ds(pl.multiple_of((j % 2) * GROUP, 128), GROUP)
        sa[1, j // 2, :, part] = dot(cbt[0], starts).astype(BF16)
        return carry

    lax.fori_loop(0, 8, prepare_adjoint, 0)

    partner = (cx, yy * 2 + 1 - core)

    def p0(j):
        return remote(sa.at[core, j], partner_sa.at[j], ps.at[j], pr.at[j], partner)

    def p0_d():
        return remote(own_d, partner_d, pds.at[0], pdr.at[0], partner)

    p0_d().start()

    @pl.when(core == 1)
    def _():
        for j in range(4):
            p0(j).start()

    loads[3].wait()
    for k in range(1, 8):
        tab_copy(k).wait_recv()

    def y1(i, k):
        to = at4((pos_y + k) % 4)
        return remote(
            tot.at[to, half(i), :], yin.at[pos_y, half(i), :], y1s.at[i, k - 1], y1r.at[i, k - 1], (cx, to * 2 + core)
        )

    def y1_d(k):
        to = at4((pos_y + k) % 4)
        return remote(tot_d.at[to], yin_d.at[pos_y], yds.at[k - 1], ydr.at[k - 1], (cx, to * 2 + core))

    def x1(i, k):
        to = at4((pos_x + k) % 4)
        return remote(
            gt.at[piece(i, to), :], xin.at[i, pos_x], x1s.at[i, k - 1], x1r.at[i, k - 1], (zz * 4 + to, hd)
        )

    def x1_d(k):
        to = at4((pos_x + k) % 4)
        return remote(gd, xin_d.at[pos_x], xds.at[k - 1], xdr.at[k - 1], (zz * 4 + to, hd))

    def z1(i, k):
        to = at8((pos_z + k) % 8)
        return remote(rt.at[i], zin.at[i, k - 1], z1s.at[i, k - 1], z1r.at[i, k - 1], (to * 4 + xx, hd))

    def z1_d(k):
        to = at8((pos_z + k) % 8)
        return remote(rd, zin_d.at[k - 1], zds.at[k - 1], zdr.at[k - 1], (to * 4 + xx, hd))

    def x2(i, k):
        to = (pos_x + k) % 4
        return remote(
            xo.at[i, to], gc.at[piece(i, xx), :], x2s.at[i, k - 1], x2r.at[i, k - 1], (zz * 4 + at4(to), hd)
        )

    def y2(i, k):
        to = (pos_y + k) % 4
        return remote(
            yo.at[to, half(i), :], w.at[yy, half(i), :], y2s.at[i, k - 1], y2r.at[i, k - 1], (cx, at4(to) * 2 + core)
        )

    def came(k):
        return at4((pos_y - k + 4) % 4)

    def p2(i, k):
        j = came(k)
        return remote(w.at[j, half(i), :], full.at[mydir, j, half(i), :], p2s.at[i, k], p2r.at[i, k], partner)

    def total(i):
        if i == 0:
            p0_d().wait_recv()
        for k in (2, 1, 3, 0):
            to = at4((pos_y + k) % 4)
            at = pl.ds(pl.multiple_of(to * SLICE, 128), SLICE)
            d = own_d[:, at]
            if i == 0:
                p0(to).wait_recv()
            value = (
                d * partner_sa[to, half(i), :].astype(F32) + sa[mydir, to, half(i), :].astype(F32)
            ).astype(BF16)
            if k:
                tot[to, half(i), :] = value
                y1(i, k).start()
            else:
                yin[pos_y, half(i), :] = value
            if i == 0:
                both = d * partner_d[:, at]
                if k:
                    tot_d[to] = both
                    y1_d(k).start()
                else:
                    yin_d[pos_y] = both

    def group_y(i):
        for k in (1, 3, 2):
            y1(i, k).wait_recv()
            if i == 0:
                y1_d(k).wait_recv()

        def chunk(n, carry):
            rows = piece(i, n)
            held = yin[0, rows, :].astype(F32)
            for p in range(1, 4):
                ypre[p - 1, rows, :] = held
                held = yin_d[p] * held + yin[p, rows, :].astype(F32)
            gt[rows, :] = held.astype(BF16)
            return carry

        lax.fori_loop(0, 4, chunk, 0)
        if i == 0:
            gd[...] = yin_d[0] * yin_d[1] * yin_d[2] * yin_d[3]
        for k in (2, 1, 3):
            x1(i, k).start()
        if i == 0:
            for k in (2, 1, 3):
                x1_d(k).start()
            xin_d[pos_x] = gd[...]
        xin[i, pos_x] = gt[piece(i, xx), :]

    def group_x(i):
        for k in (1, 3, 2):
            x1(i, k).wait_recv()
            if i == 0:
                x1_d(k).wait_recv()
        held = xin[i, 0].astype(F32)
        for p in range(1, 4):
            xpre[i, p - 1] = held
            held = xin_d[p] * held + xin[i, p].astype(F32)
        rt[i] = held.astype(BF16)
        if i == 0:
            rd[...] = xin_d[0] * xin_d[1] * xin_d[2] * xin_d[3]
        if i == 0:
            pl.semaphore_wait(ready, 2)
        for k in (4, 3, 5, 2, 6, 1, 7):

            @pl.when(pos_z + k < 8)
            def _():
                z1(i, k).start()
                if i == 0:
                    z1_d(k).start()

    def back_x(i):
        for k in range(1, 8):

            @pl.when(pos_z >= k)
            def _():
                z1(i, k).wait_recv()
                if i == 0:
                    z1_d(k).wait_recv()

        held = zin[i, 0].astype(F32)
        weight = zin_d[0]
        for k in range(1, 7):
            held = held + weight * zin[i, k].astype(F32)
            weight = weight * zin_d[k]
        xo[i, 0] = held.astype(BF16)
        prod = xin_d[0]
        for p in range(1, 4):
            xo[i, p] = (prod * held + xpre[i, p - 1]).astype(BF16)
            prod = prod * xin_d[p]
        for k in (2, 1, 3):
            x2(i, k).start()
        gc[piece(i, xx), :] = xo[i, pos_x]

    def back_y(i):
        for k in (1, 3, 2):
            x2(i, k).wait_recv()

        def chunk(n, carry):
            rows = piece(i, n)
            base = gc[rows, :].astype(F32)
            yo[0, rows, :] = gc[rows, :]
            prod = yin_d[0]
            for p in range(1, 4):
                yo[p, rows, :] = (prod * base + ypre[p - 1, rows, :]).astype(BF16)
                prod = prod * yin_d[p]
            return carry

        lax.fori_loop(0, 4, chunk, 0)
        for k in (2, 1, 3):
            y2(i, k).start()
        w[yy, half(i), :] = yo[pos_y, half(i), :]

    def arrive(i, k):
        if k:
            y2(i, k).wait_recv()
        p2(i, k).start()
        j = came(k)
        at = pl.ds(pl.multiple_of(j * SLICE, 128), SLICE)
        full[mydir, j, half(i), :] = (
            partner_d[:, at] * w[j, half(i), :].astype(F32) + partner_sa[j, half(i), :].astype(F32)
        ).astype(BF16)

    def finish(way, j):
        at = pl.ds(pl.multiple_of(j * SLICE, 128), SLICE)
        carried = full[way, j]
        out[way, :, at] = (loc[way, :, at] + wts[way, :, at] * dot(cb[way], carried)).astype(BF16)
        acc[way] += dot_nt(gi[way, :, at], carried)

    @pl.when(core == 0)
    def _():
        total(0)
        total(1)

    def prepare_state(n, carry):
        turn = n // 2
        step = jnp.where(turn == 0, 2, jnp.where(turn == 1, 1, jnp.where(turn == 2, 3, 0)))
        j = (yy + step) % 4
        group = j * 2 + n % 2
        cols = columns(group)
        inputs = (x[:, cols].astype(F32) + dot(onehot[...], tab[group])).astype(BF16)
        u[:, cols] = inputs
        ends = (dot(wcat[1], spread[:, cols]) * inputs.astype(F32)).astype(BF16)
        part = pl.ds(pl.multiple_of((n % 2) * GROUP, 128), GROUP)
        sa[0, j, :, part] = dot(cbt[1], ends).astype(BF16)

        @pl.when((core == 0) & (n % 2 == 1))
        def _():
            p0(j).start()

        return carry

    lax.fori_loop(0, 8, prepare_state, 0)

    @pl.when(core == 1)
    def _():
        total(0)
        total(1)

    lane = lax.broadcasted_iota(jnp.int32, (TOK, 128), 1)
    first = lane < 64

    def intra(j, carry):
        for adjoint_at, state_at, act, part in (
            (2, 4, group_y, 0),
            (4, 6, group_y, 1),
            (4, 6, group_x, 0),
            (6, 8, group_x, 1),
        ):
            pl.when(j == core * state_at + mydir * adjoint_at)(functools.partial(act, part))
        pl.when(j < 8)(functools.partial(local, j))
        return carry

    def local(j):
        rows_l = logs[j]
        cols_l = jnp.transpose(rows_l)
        for pair in range(3):
            cols = pl.ds(pl.multiple_of(j * GROUP + pair * 128, 128), 128)
            up = u[:, cols]
            gp = g[:, cols]
            for way, values in ((0, gp), (1, up)):
                weight = dot(wcat[way], spread[:, cols])
                wts[way, :, cols] = weight
                gi[way, :, cols] = (weight * values.astype(F32)).astype(BF16)
            zero = jnp.zeros_like(gp)
            ys, dus = [], []
            for side in range(2):
                r = pair * 2 + side
                lr = rows_l[r : r + 1, :]
                lc = cols_l[:, r : r + 1]
                gm = jnp.where(first, gp, zero) if side == 0 else jnp.where(first, zero, gp)
                da = jnp.exp2(jnp.minimum(lc[:128] - lr[:, :128], 0.0))
                mix_a = (da * cbm[:128, :128]).astype(BF16)
                paired[:128, :128] += da * dot_nt(gm[:128], up[:128])
                db = jnp.exp2(jnp.minimum(lc[128:] - lr, 0.0))
                mix_b = (db * cbm[128:, :]).astype(BF16)
                paired[128:, :] += db * dot_nt(gm[128:], up)
                ys.append((dot(mix_a, up[:128]), dot(mix_b, up)))
                low = dot_tn(mix_b, gp[128:])
                dus.append((low[:128] + dot_tn(mix_a, gp[:128]), low[128:]))
            s0 = skip_ref[j * 6 + pair * 2]
            s1 = skip_ref[j * 6 + pair * 2 + 1]
            scale = jnp.where(first[:128], s0, s1)
            for part in range(2):
                at = slice(part * 128, part * 128 + 128)
                loc[0, at, cols] = jnp.where(first[at], ys[0][part], ys[1][part]) + scale * up[at].astype(F32)
                loc[1, at, cols] = jnp.where(first[at], dus[0][part], dus[1][part]) + scale * gp[at].astype(F32)

    lax.fori_loop(0, 9, intra, 0)

    pairs = (paired[...] * vis[...]).astype(BF16)
    acc[0] = dot(pairs, cb[1])
    acc[1] = dot_tn(pairs, cb[0])

    back_x(0)
    back_x(1)
    back_y(0)
    back_y(1)

    def carried_here(way):
        for k in range(4):
            arrive(0, k)
        for k in range(4):
            arrive(1, k)
            finish(way, came(k))

    def carried_there(way):
        for k in range(4):
            p2(0, k).wait_recv()
            p2(1, k).wait_recv()
            finish(way, at4((pos_y + k) % 4))

    @pl.when(core == 0)
    def _():
        carried_here(1)
        carried_there(0)

    @pl.when(core == 1)
    def _():
        carried_there(1)
        carried_here(0)

    proj_out[...] = acc[...].astype(BF16)

    for k in range(1, 8):
        ld_copy(k).wait_send()
        tab_copy(k).wait_send()

        @pl.when(pos_z + k < 8)
        def _():
            z1_d(k).wait_send()
            for i in range(CHUNKS):
                z1(i, k).wait_send()

    p0_d().wait_send()
    for k in range(1, 4):
        y1_d(k).wait_send()
        x1_d(k).wait_send()
    for j in range(4):
        p0(j).wait_send()
    for i in range(CHUNKS):
        for k in range(1, 4):
            for make in (y1, x1, x2, y2):
                make(i, k).wait_send()
        for k in range(4):
            p2(i, k).wait_send()


def store_kernel(values, proj, y_out, du_out, db_out, dc_out, sem):
    moves = ((values.at[0], y_out), (values.at[1], du_out), (proj.at[1], db_out), (proj.at[0], dc_out))
    copies = [pltpu.make_async_copy(src, dst, sem.at[i]) for i, (src, dst) in enumerate(moves)]
    for one in copies:
        one.start()
    for one in copies:
        one.wait()


def body(layer_input, cotangent, b_proj, c_proj, log_decay, resets, agent_ids, skip_gain, agent_table):
    dma = pltpu.SemaphoreType.DMA
    vm = pltpu.VMEM
    any_spec = pl.BlockSpec(memory_space=pl.ANY)
    vmem_spec = pl.BlockSpec(memory_space=pltpu.VMEM)
    wide = (TOK, FEAT)
    n = CHUNKS
    hbm = [
        pltpu.with_memory_space_constraint(a, pltpu.HBM)
        for a in (layer_input, cotangent, b_proj, c_proj, log_decay.T, agent_table)
    ]
    values, proj = pl.pallas_call(
        kernel,
        out_shape=(vm((2, TOK, FEAT), BF16), vm((2, TOK, STATE), BF16)),
        in_specs=[any_spec] * 6 + [vmem_spec] * 2 + [pl.BlockSpec(memory_space=pltpu.SMEM)],
        out_specs=(vmem_spec, vmem_spec),
        scratch_shapes=[
            vm(wide, BF16), vm(wide, BF16), vm((2, TOK, STATE), BF16), vm((2, STATE, TOK), BF16),
            vm((8, 8, TOK), F32), vm((8, 64, GROUP), BF16), vm((8, 8, TOK), F32),
            vm((TOK, TOK), F32), vm((TOK, TOK), F32), vm((TOK, TOK), F32),
            vm((TOK, 64), BF16), vm((2, TOK, 192), BF16), vm((192, FEAT), BF16),
            vm(wide, BF16), vm((2, TOK, FEAT), BF16), vm((2, TOK, FEAT), F32), vm((2, TOK, FEAT), F32),
            vm((2, TOK, STATE), F32),
            vm((2, 4, STATE, SLICE), BF16), vm((1, FEAT), F32), vm((4, STATE, SLICE), BF16), vm((1, FEAT), F32),
            vm((4, STATE, SLICE), BF16), vm((4, 1, SLICE), F32),
            vm((4, STATE, SLICE), BF16), vm((4, 1, SLICE), F32), vm((3, STATE, SLICE), F32),
            vm((STATE, SLICE), BF16), vm((1, SLICE), F32),
            vm((n, 4, PIECE, SLICE), BF16), vm((4, 1, SLICE), F32), vm((n, 3, PIECE, SLICE), F32),
            vm((n, PIECE, SLICE), BF16), vm((1, SLICE), F32),
            vm((n, 7, PIECE, SLICE), BF16), vm((7, 1, SLICE), F32),
            vm((n, 4, PIECE, SLICE), BF16), vm((STATE, SLICE), BF16),
            vm((4, STATE, SLICE), BF16), vm((4, STATE, SLICE), BF16), vm((2, 4, STATE, SLICE), BF16),
            dma((6,)), dma((2, 7)), dma((2, 7)), dma((4,)), dma((4,)), dma((1,)), dma((1,)),
            dma((n, 3)), dma((n, 3)), dma((3,)), dma((3,)),
            dma((n, 3)), dma((n, 3)), dma((3,)), dma((3,)),
            dma((n, 7)), dma((n, 7)), dma((7,)), dma((7,)),
            dma((n, 3)), dma((n, 3)), dma((n, 3)), dma((n, 3)), dma((n, 4)), dma((n, 4)),
            pltpu.SemaphoreType.REGULAR, vm((6, 8 * TOK), F32),
        ],
        compiler_params=pltpu.CompilerParams(
            collective_id=0, has_side_effects=True, vmem_limit_bytes=56 * 1024 * 1024
        ),
        name="tract_scan",
    )(*hbm, resets.reshape(1, -1), agent_ids.reshape(1, -1), skip_gain)
    token = jax.ShapeDtypeStruct(wide, BF16)
    narrow = jax.ShapeDtypeStruct((TOK, STATE), BF16)
    return pl.pallas_call(
        store_kernel,
        out_shape=(token, token, narrow, narrow),
        in_specs=[any_spec] * 2,
        out_specs=(any_spec,) * 4,
        scratch_shapes=[dma((4,))],
        name="store",
    )(pltpu.with_memory_space_constraint(values, vm), pltpu.with_memory_space_constraint(proj, vm))


def solution(mesh):
    return jax.shard_map(
        body,
        mesh=mesh,
        in_specs=(
            P(("ctx", "head"), None),
            P(("ctx", "head"), None),
            P("ctx", None),
            P("ctx", None),
            P("ctx", "head"),
            P("ctx"),
            P("ctx"),
            P(),
            P(None, "head"),
        ),
        out_specs=(P(("ctx", "head"), None),) * 4,
        check_vma=False,
    )
```

```python
import functools

import jax
import jax.numpy as jnp
from jax import lax
from jax.experimental import pallas as pl
from jax.experimental.pallas import tpu as pltpu
from jax.sharding import PartitionSpec as P

MESH = pl.DeviceIdType.MESH
F32 = jnp.float32
BF16 = jnp.bfloat16
TOK = 256
FEAT = 3072
STATE = 128
GROUP = 384
SLICE = 768
HALF = 64
PIECE = 16
CHUNKS = 2
ADJOINT_AT = (1, 3, 2, 4, 5, 5, 6, 6)
STATE_AT = (2, 4, 3, 5, 6, 7, 7, 8)
LOG2E = 1.4426950408889634


def dot(a, b):
    return jnp.dot(a, b, preferred_element_type=F32)


def dot_nt(a, b):
    return lax.dot_general(a, b, (((1,), (1,)), ((), ())), preferred_element_type=F32)


def dot_tn(a, b):
    return lax.dot_general(a, b, (((0,), (0,)), ((), ())), preferred_element_type=F32)


def split3(a):
    hi = a.astype(BF16)
    rest = a - hi.astype(F32)
    mid = rest.astype(BF16)
    low = (rest - mid.astype(F32)).astype(BF16)
    return hi, mid, low


def kernel(
    x_hbm, g_hbm, b_hbm, c_hbm, ld_hbm, tab_hbm, resets_ref, ids_ref, skip_ref,
    out, proj_out,
    x, g, cb, cbt, ld, tab, logs, cbm, vis, paired, onehot, wcat, spread,
    u, gi, wts, loc, acc, sa, own_d, partner_sa, partner_d,
    tot, tot_d, yin, yin_d, ypre, gt, gd, xin, xin_d, xpre, rt, rd, zin, zin_d,
    xo, gc, yo, w, full,
    lsem, hs, hr, ps, pr, pds, pdr, y1s, y1r, yds, ydr, x1s, x1r, xds, xdr, z1s, z1r, zds, zdr,
    x2s, x2r, y2s, y2r, p2s, p2r, ready, ld_own,
):
    cx = lax.axis_index("ctx")
    hd = lax.axis_index("head")
    zz, xx = cx // 4, cx % 4
    yy, core = hd // 2, hd % 2
    mydir = 1 - core
    pos_y = core * yy + (1 - core) * (3 - yy)
    pos_x = core * xx + (1 - core) * (3 - xx)
    pos_z = core * zz + (1 - core) * (7 - zz)

    def at4(q):
        return core * q + (1 - core) * (3 - q)

    def at8(q):
        return core * q + (1 - core) * (7 - q)

    def remote(src, dst, s, r, dev):
        return pltpu.make_async_remote_copy(
            src_ref=src, dst_ref=dst, send_sem=s, recv_sem=r, device_id=dev, device_id_type=MESH
        )

    def half(i):
        return pl.ds(i * HALF, HALF)

    def piece(i, place):
        return pl.ds(pl.multiple_of(i * HALF + place * PIECE, PIECE), PIECE)

    ld[:, 6:8, :] = jnp.zeros((8, 2, TOK), F32)
    zin_d[...] = jnp.zeros_like(zin_d)
    zin[...] = jnp.zeros_like(zin)

    barrier = pltpu.get_barrier_semaphore()
    for k in (2, 6, 1, 7):
        pl.semaphore_signal(barrier, inc=1, device_id=(((zz + k) % 8) * 4 + xx, hd), device_id_type=MESH)
    for k in range(1, 8):
        pl.semaphore_signal(barrier, inc=1, device_id=(cx, (hd + k) % 8), device_id_type=MESH)
    for k in range(1, 4):
        pl.semaphore_signal(barrier, inc=1, device_id=(zz * 4 + (xx + k) % 4, hd), device_id_type=MESH)

    mine = pl.ds(pl.multiple_of(hd * TOK, TOK), TOK)
    own_ld = pltpu.make_async_copy(ld_hbm, ld_own, lsem.at[5])
    loads = [
        pltpu.make_async_copy(g_hbm, g, lsem.at[0]),
        pltpu.make_async_copy(b_hbm.at[mine, :], cb.at[1], lsem.at[1]),
        pltpu.make_async_copy(c_hbm.at[mine, :], cb.at[0], lsem.at[2]),
        pltpu.make_async_copy(x_hbm, x, lsem.at[3]),
    ]
    own_tab = pltpu.make_async_copy(tab_hbm, tab.at[hd], lsem.at[4])
    own_ld.start()
    own_tab.start()
    for one in (loads[1], loads[2], loads[0], loads[3]):
        one.start()

    paired[...] = jnp.zeros_like(paired)

    def build(j, carry):
        r3 = lax.broadcasted_iota(jnp.int32, (192, GROUP), 0)
        c3 = lax.broadcasted_iota(jnp.int32, (192, GROUP), 1)
        spread[:, pl.ds(pl.multiple_of(j * GROUP, 128), GROUP)] = (
            ((r3 & 63) == 8 * j + (c3 >> 6)).astype(F32).astype(BF16)
        )
        return carry

    lax.fori_loop(0, 8, build, 0)
    own_ld.wait()
    own_tab.wait()
    pl.semaphore_wait(barrier, 14)

    def ld_copy(k):
        to = (hd + k) % 8
        theirs = pl.ds(pl.multiple_of(to * TOK, TOK), TOK)
        return remote(
            ld_own.at[:, theirs], ld.at[hd, pl.ds(0, 6), :], hs.at[0, k - 1], hr.at[0, k - 1], (cx, to)
        )

    def tab_copy(k):
        return remote(tab.at[hd], tab.at[hd], hs.at[1, k - 1], hr.at[1, k - 1], (cx, (hd + k) % 8))

    for k in (4, 3, 5, 2, 6, 1, 7):
        ld_copy(k).start()
    for k in (4, 3, 5, 2, 6, 1, 7):
        tab_copy(k).start()
    for k in (2, 6):
        pl.semaphore_signal(ready, inc=1, device_id=(((zz + k) % 8) * 4 + xx, hd), device_id_type=MESH)
    ld[hd, 0:6, :] = ld_own[:, mine]

    row = lax.broadcasted_iota(jnp.int32, (TOK, TOK), 0)
    col = lax.broadcasted_iota(jnp.int32, (TOK, TOK), 1)
    upper = (row <= col).astype(F32).astype(BF16)
    flags = resets_ref[:, mine].astype(F32)
    seen = dot(jnp.broadcast_to(flags, (8, TOK)).astype(BF16), upper)
    seen_row = seen[0:1, :]
    seen_col = jnp.transpose(seen)[:, 0:1]
    visible = ((col <= row) & (seen_row == seen_col)).astype(F32)
    vis[...] = visible
    loads[1].wait()
    loads[2].wait()
    cbm[...] = dot_nt(cb[0], cb[1]) * visible
    cbt[0] = jnp.transpose(cb[0].astype(F32)).astype(BF16)
    cbt[1] = jnp.transpose(cb[1].astype(F32)).astype(BF16)
    agent = lax.broadcasted_iota(jnp.int32, (64, TOK), 0)
    picked = (agent == ids_ref[:, mine]).astype(F32)
    onehot[...] = jnp.transpose(picked).astype(BF16)

    for k in range(1, 8):
        ld_copy(k).wait_recv()
    hi, mid, low = split3(ld[...].reshape(64, TOK))
    run = (dot(hi, upper) + dot(mid, upper) + dot(low, upper)) * LOG2E
    logs[...] = run.reshape(8, 8, TOK)
    run_end = run[:, TOK - 1 : TOK]
    seen_end = seen_row[:, TOK - 1 : TOK]
    start = jnp.where(seen_row == 0, jnp.exp2(run), 0.0)
    end = jnp.where(seen_row == seen_end, jnp.exp2(jnp.minimum(run_end - run, 0.0)), 0.0)
    for index, value in ((0, start), (1, end)):
        turned = jnp.transpose(value)
        wcat[index] = jnp.concatenate(split3(turned), axis=1)

    loads[0].wait()

    def columns(j):
        return pl.ds(pl.multiple_of(j * GROUP, 128), GROUP)

    def slice_columns(j):
        return pl.ds(pl.multiple_of(j * SLICE, 128), SLICE)

    def prepare_adjoint(j, carry):
        cols = slice_columns(j)
        weight = dot(wcat[0], spread[:, cols])
        own_d[:, cols] = weight[TOK - 1 : TOK, :]
        starts = (weight * g[:, cols].astype(F32)).astype(BF16)
        sa[1, j] = dot(cbt[0], starts).astype(BF16)
        return carry

    lax.fori_loop(0, 4, prepare_adjoint, 0)

    partner = (cx, yy * 2 + 1 - core)

    def p0(j):
        return remote(sa.at[core, j], partner_sa.at[j], ps.at[j], pr.at[j], partner)

    def p0_d():
        return remote(own_d, partner_d, pds.at[0], pdr.at[0], partner)

    p0_d().start()

    @pl.when(core == 1)
    def _():
        for j in range(4):
            p0(j).start()

    loads[3].wait()
    for k in range(1, 8):
        tab_copy(k).wait_recv()

    def y1(i, k):
        to = at4((pos_y + k) % 4)
        return remote(
            tot.at[to, half(i), :], yin.at[pos_y, half(i), :], y1s.at[i, k - 1], y1r.at[i, k - 1], (cx, to * 2 + core)
        )

    def y1_d(k):
        to = at4((pos_y + k) % 4)
        return remote(tot_d.at[to], yin_d.at[pos_y], yds.at[k - 1], ydr.at[k - 1], (cx, to * 2 + core))

    def x1(i, k):
        to = at4((pos_x + k) % 4)
        return remote(
            gt.at[piece(i, to), :], xin.at[i, pos_x], x1s.at[i, k - 1], x1r.at[i, k - 1], (zz * 4 + to, hd)
        )

    def x1_d(k):
        to = at4((pos_x + k) % 4)
        return remote(gd, xin_d.at[pos_x], xds.at[k - 1], xdr.at[k - 1], (zz * 4 + to, hd))

    def z1(i, k):
        to = at8((pos_z + k) % 8)
        return remote(rt.at[i], zin.at[i, k - 1], z1s.at[i, k - 1], z1r.at[i, k - 1], (to * 4 + xx, hd))

    def z1_d(k):
        to = at8((pos_z + k) % 8)
        return remote(rd, zin_d.at[k - 1], zds.at[k - 1], zdr.at[k - 1], (to * 4 + xx, hd))

    def x2(i, k):
        to = (pos_x + k) % 4
        return remote(
            xo.at[i, to], gc.at[piece(i, xx), :], x2s.at[i, k - 1], x2r.at[i, k - 1], (zz * 4 + at4(to), hd)
        )

    def y2(i, k):
        to = (pos_y + k) % 4
        return remote(
            yo.at[to, half(i), :], w.at[yy, half(i), :], y2s.at[i, k - 1], y2r.at[i, k - 1], (cx, at4(to) * 2 + core)
        )

    def came(k):
        return at4((pos_y - k + 4) % 4)

    def p2(i, k):
        j = came(k)
        return remote(w.at[j, half(i), :], full.at[mydir, j, half(i), :], p2s.at[i, k], p2r.at[i, k], partner)

    def total(i):
        if i == 0:
            p0_d().wait_recv()
        for k in (2, 1, 3, 0):
            to = at4((pos_y + k) % 4)
            at = pl.ds(pl.multiple_of(to * SLICE, 128), SLICE)
            d = own_d[:, at]
            if i == 0:
                p0(to).wait_recv()
            value = (
                d * partner_sa[to, half(i), :].astype(F32) + sa[mydir, to, half(i), :].astype(F32)
            ).astype(BF16)
            if k:
                tot[to, half(i), :] = value
                y1(i, k).start()
            else:
                yin[pos_y, half(i), :] = value
            if i == 0:
                both = d * partner_d[:, at]
                if k:
                    tot_d[to] = both
                    y1_d(k).start()
                else:
                    yin_d[pos_y] = both

    def group_y(i):
        for k in (1, 3, 2):
            y1(i, k).wait_recv()
            if i == 0:
                y1_d(k).wait_recv()

        def chunk(n, carry):
            rows = piece(i, n)
            held = yin[0, rows, :].astype(F32)
            for p in range(1, 4):
                ypre[p - 1, rows, :] = held
                held = yin_d[p] * held + yin[p, rows, :].astype(F32)
            gt[rows, :] = held.astype(BF16)
            return carry

        lax.fori_loop(0, 4, chunk, 0)
        if i == 0:
            gd[...] = yin_d[0] * yin_d[1] * yin_d[2] * yin_d[3]
        for k in (2, 1, 3):
            x1(i, k).start()
        if i == 0:
            for k in (2, 1, 3):
                x1_d(k).start()
            xin_d[pos_x] = gd[...]
        xin[i, pos_x] = gt[piece(i, xx), :]

    def group_x(i):
        for k in (1, 3, 2):
            x1(i, k).wait_recv()
            if i == 0:
                x1_d(k).wait_recv()
        held = xin[i, 0].astype(F32)
        for p in range(1, 4):
            xpre[i, p - 1] = held
            held = xin_d[p] * held + xin[i, p].astype(F32)
        rt[i] = held.astype(BF16)
        if i == 0:
            rd[...] = xin_d[0] * xin_d[1] * xin_d[2] * xin_d[3]
        if i == 0:
            pl.semaphore_wait(ready, 2)
        for k in (4, 3, 5, 2, 6, 1, 7):

            @pl.when(pos_z + k < 8)
            def _():
                z1(i, k).start()
                if i == 0:
                    z1_d(k).start()

    def back_x(i):
        for k in range(1, 8):

            @pl.when(pos_z >= k)
            def _():
                z1(i, k).wait_recv()
                if i == 0:
                    z1_d(k).wait_recv()

        held = zin[i, 0].astype(F32)
        weight = zin_d[0]
        for k in range(1, 7):
            held = held + weight * zin[i, k].astype(F32)
            weight = weight * zin_d[k]
        xo[i, 0] = held.astype(BF16)
        prod = xin_d[0]
        for p in range(1, 4):
            xo[i, p] = (prod * held + xpre[i, p - 1]).astype(BF16)
            prod = prod * xin_d[p]
        for k in (2, 1, 3):
            x2(i, k).start()
        gc[piece(i, xx), :] = xo[i, pos_x]

    def back_y(i):
        for k in (1, 3, 2):
            x2(i, k).wait_recv()

        def chunk(n, carry):
            rows = piece(i, n)
            base = gc[rows, :].astype(F32)
            yo[0, rows, :] = gc[rows, :]
            prod = yin_d[0]
            for p in range(1, 4):
                yo[p, rows, :] = (prod * base + ypre[p - 1, rows, :]).astype(BF16)
                prod = prod * yin_d[p]
            return carry

        lax.fori_loop(0, 4, chunk, 0)
        for k in (2, 1, 3):
            y2(i, k).start()
        w[yy, half(i), :] = yo[pos_y, half(i), :]

    def forward(i):
        for k in (0, 1, 3, 2):
            if k:
                y2(i, k).wait_recv()
            p2(i, k).start()

    def own_carry(i, k):
        j = came(k)
        at = pl.ds(pl.multiple_of(j * SLICE, 128), SLICE)
        full[mydir, j, half(i), :] = (
            partner_d[:, at] * w[j, half(i), :].astype(F32) + partner_sa[j, half(i), :].astype(F32)
        ).astype(BF16)

    def finish(way, j):
        at = pl.ds(pl.multiple_of(j * SLICE, 128), SLICE)
        carried = full[way, j]
        out[way, :, at] = (loc[way, :, at] + wts[way, :, at] * dot(cb[way], carried)).astype(BF16)
        acc[way] += dot_nt(gi[way, :, at], carried)

    @pl.when(core == 0)
    def _():
        total(0)
        total(1)

    def prepare_state(turn, carry):
        step = jnp.where(turn == 0, 2, jnp.where(turn == 1, 1, jnp.where(turn == 2, 3, 0)))
        j = (yy + step) % 4
        cols = slice_columns(j)
        rows = jnp.concatenate([tab[j * 2], tab[j * 2 + 1]], axis=1)
        inputs = (x[:, cols].astype(F32) + dot(onehot[...], rows)).astype(BF16)
        u[:, cols] = inputs
        ends = (dot(wcat[1], spread[:, cols]) * inputs.astype(F32)).astype(BF16)
        sa[0, j] = dot(cbt[1], ends).astype(BF16)

        @pl.when(core == 0)
        def _():
            p0(j).start()

        return carry

    lax.fori_loop(0, 4, prepare_state, 0)

    @pl.when(core == 1)
    def _():
        total(0)
        total(1)

    lane = lax.broadcasted_iota(jnp.int32, (TOK, 128), 1)
    first = lane < 64

    def intra(j, carry):
        for adjoint_at, state_at, act, part in (
            (ADJOINT_AT[0], STATE_AT[0], group_y, 0),
            (ADJOINT_AT[1], STATE_AT[1], group_x, 0),
            (ADJOINT_AT[2], STATE_AT[2], group_y, 1),
            (ADJOINT_AT[3], STATE_AT[3], group_x, 1),
            (ADJOINT_AT[4], STATE_AT[4], back_x, 0),
            (ADJOINT_AT[5], STATE_AT[5], back_x, 1),
            (ADJOINT_AT[6], STATE_AT[6], back_y, 0),
            (ADJOINT_AT[7], STATE_AT[7], back_y, 1),
        ):
            pl.when(j == core * state_at + mydir * adjoint_at)(functools.partial(act, part))
        pl.when(j < 8)(functools.partial(local, j))
        return carry

    def local(j):
        rows_l = logs[j]
        cols_l = jnp.transpose(rows_l)
        wide = columns(j)
        for way, values in ((0, g), (1, u)):
            weight = dot(wcat[way], spread[:, wide])
            wts[way, :, wide] = weight
            gi[way, :, wide] = (weight * values[:, wide].astype(F32)).astype(BF16)
        for pair in range(3):
            cols = pl.ds(pl.multiple_of(j * GROUP + pair * 128, 128), 128)
            up = u[:, cols]
            gp = g[:, cols]
            zero = jnp.zeros_like(gp)
            ys, dus = [], []
            for side in range(2):
                r = pair * 2 + side
                lr = rows_l[r : r + 1, :]
                lc = cols_l[:, r : r + 1]
                gm = jnp.where(first, gp, zero) if side == 0 else jnp.where(first, zero, gp)
                da = jnp.exp2(jnp.minimum(lc[:128] - lr[:, :128], 0.0))
                mix_a = (da * cbm[:128, :128]).astype(BF16)
                paired[:128, :128] += da * dot_nt(gm[:128], up[:128])
                db = jnp.exp2(jnp.minimum(lc[128:] - lr, 0.0))
                mix_b = (db * cbm[128:, :]).astype(BF16)
                paired[128:, :] += db * dot_nt(gm[128:], up)
                ys.append((dot(mix_a, up[:128]), dot(mix_b, up)))
                low = dot_tn(mix_b, gp[128:])
                dus.append((low[:128] + dot_tn(mix_a, gp[:128]), low[128:]))
            s0 = skip_ref[j * 6 + pair * 2]
            s1 = skip_ref[j * 6 + pair * 2 + 1]
            scale = jnp.where(first[:128], s0, s1)
            for part in range(2):
                at = slice(part * 128, part * 128 + 128)
                loc[0, at, cols] = jnp.where(first[at], ys[0][part], ys[1][part]) + scale * up[at].astype(F32)
                loc[1, at, cols] = jnp.where(first[at], dus[0][part], dus[1][part]) + scale * gp[at].astype(F32)

    lax.fori_loop(0, 9, intra, 0)

    pairs = (paired[...] * vis[...]).astype(BF16)
    acc[0] = dot(pairs, cb[1])
    acc[1] = dot_tn(pairs, cb[0])

    def carried_here(way):
        forward(0)
        for k in range(4):
            own_carry(0, k)
        forward(1)
        for k in (0, 1, 3, 2):
            own_carry(1, k)
            finish(way, came(k))

    def carried_there(way):
        for k in (0, 1, 3, 2):
            p2(0, k).wait_recv()
            p2(1, k).wait_recv()
            finish(way, at4((pos_y + k) % 4))

    @pl.when(core == 0)
    def _():
        carried_here(1)
        carried_there(0)

    @pl.when(core == 1)
    def _():
        carried_there(1)
        carried_here(0)

    proj_out[...] = acc[...].astype(BF16)

    for k in range(1, 8):
        ld_copy(k).wait_send()
        tab_copy(k).wait_send()

        @pl.when(pos_z + k < 8)
        def _():
            z1_d(k).wait_send()
            for i in range(CHUNKS):
                z1(i, k).wait_send()

    p0_d().wait_send()
    for k in range(1, 4):
        y1_d(k).wait_send()
        x1_d(k).wait_send()
    for j in range(4):
        p0(j).wait_send()
    for i in range(CHUNKS):
        for k in range(1, 4):
            for make in (y1, x1, x2, y2):
                make(i, k).wait_send()
        for k in range(4):
            p2(i, k).wait_send()


def store_kernel(values, proj, y_out, du_out, db_out, dc_out, sem):
    moves = [(proj.at[1], db_out), (proj.at[0], dc_out)]
    for part in range(4):
        rows = pl.ds(part * 64, 64)
        moves += [(values.at[0, rows], y_out.at[rows]), (values.at[1, rows], du_out.at[rows])]
    copies = [pltpu.make_async_copy(src, dst, sem.at[i]) for i, (src, dst) in enumerate(moves)]
    for one in copies:
        one.start()
    for one in copies:
        one.wait()


def body(layer_input, cotangent, b_proj, c_proj, log_decay, resets, agent_ids, skip_gain, agent_table):
    dma = pltpu.SemaphoreType.DMA
    vm = pltpu.VMEM
    any_spec = pl.BlockSpec(memory_space=pl.ANY)
    vmem_spec = pl.BlockSpec(memory_space=pltpu.VMEM)
    wide = (TOK, FEAT)
    n = CHUNKS
    hbm = [
        pltpu.with_memory_space_constraint(a, pltpu.HBM)
        for a in (layer_input, cotangent, b_proj, c_proj, log_decay.T, agent_table)
    ]
    values, proj = pl.pallas_call(
        kernel,
        out_shape=(vm((2, TOK, FEAT), BF16), vm((2, TOK, STATE), BF16)),
        in_specs=[any_spec] * 6 + [vmem_spec] * 2 + [pl.BlockSpec(memory_space=pltpu.SMEM)],
        out_specs=(vmem_spec, vmem_spec),
        scratch_shapes=[
            vm(wide, BF16), vm(wide, BF16), vm((2, TOK, STATE), BF16), vm((2, STATE, TOK), BF16),
            vm((8, 8, TOK), F32), vm((8, 64, GROUP), BF16), vm((8, 8, TOK), F32),
            vm((TOK, TOK), F32), vm((TOK, TOK), F32), vm((TOK, TOK), F32),
            vm((TOK, 64), BF16), vm((2, TOK, 192), BF16), vm((192, FEAT), BF16),
            vm(wide, BF16), vm((2, TOK, FEAT), BF16), vm((2, TOK, FEAT), F32), vm((2, TOK, FEAT), F32),
            vm((2, TOK, STATE), F32),
            vm((2, 4, STATE, SLICE), BF16), vm((1, FEAT), F32), vm((4, STATE, SLICE), BF16), vm((1, FEAT), F32),
            vm((4, STATE, SLICE), BF16), vm((4, 1, SLICE), F32),
            vm((4, STATE, SLICE), BF16), vm((4, 1, SLICE), F32), vm((3, STATE, SLICE), F32),
            vm((STATE, SLICE), BF16), vm((1, SLICE), F32),
            vm((n, 4, PIECE, SLICE), BF16), vm((4, 1, SLICE), F32), vm((n, 3, PIECE, SLICE), F32),
            vm((n, PIECE, SLICE), BF16), vm((1, SLICE), F32),
            vm((n, 7, PIECE, SLICE), BF16), vm((7, 1, SLICE), F32),
            vm((n, 4, PIECE, SLICE), BF16), vm((STATE, SLICE), BF16),
            vm((4, STATE, SLICE), BF16), vm((4, STATE, SLICE), BF16), vm((2, 4, STATE, SLICE), BF16),
            dma((6,)), dma((2, 7)), dma((2, 7)), dma((4,)), dma((4,)), dma((1,)), dma((1,)),
            dma((n, 3)), dma((n, 3)), dma((3,)), dma((3,)),
            dma((n, 3)), dma((n, 3)), dma((3,)), dma((3,)),
            dma((n, 7)), dma((n, 7)), dma((7,)), dma((7,)),
            dma((n, 3)), dma((n, 3)), dma((n, 3)), dma((n, 3)), dma((n, 4)), dma((n, 4)),
            pltpu.SemaphoreType.REGULAR, vm((6, 8 * TOK), F32),
        ],
        compiler_params=pltpu.CompilerParams(
            collective_id=0, has_side_effects=True, vmem_limit_bytes=56 * 1024 * 1024
        ),
        name="tract_scan",
    )(*hbm, resets.reshape(1, -1), agent_ids.reshape(1, -1), skip_gain)
    token = jax.ShapeDtypeStruct(wide, BF16)
    narrow = jax.ShapeDtypeStruct((TOK, STATE), BF16)
    return pl.pallas_call(
        store_kernel,
        out_shape=(token, token, narrow, narrow),
        in_specs=[any_spec] * 2,
        out_specs=(any_spec,) * 4,
        scratch_shapes=[dma((10,))],
        name="store",
    )(pltpu.with_memory_space_constraint(values, vm), pltpu.with_memory_space_constraint(proj, vm))


def solution(mesh):
    return jax.shard_map(
        body,
        mesh=mesh,
        in_specs=(
            P(("ctx", "head"), None),
            P(("ctx", "head"), None),
            P("ctx", None),
            P("ctx", None),
            P("ctx", "head"),
            P("ctx"),
            P("ctx"),
            P(),
            P(None, "head"),
        ),
        out_specs=(P(("ctx", "head"), None),) * 4,
        check_vma=False,
    )
```

```python
import functools

import jax
import jax.numpy as jnp
from jax import lax
from jax.experimental import pallas as pl
from jax.experimental.pallas import tpu as pltpu
from jax.sharding import PartitionSpec as P

MESH = pl.DeviceIdType.MESH
F32 = jnp.float32
BF16 = jnp.bfloat16
TOK = 256
FEAT = 3072
STATE = 128
GROUP = 384
SLICE = 768
HALF = 64
PIECE = 16
CHUNKS = 2
ADJOINT_AT = (1, 3, 2, 5, 5, 6, 6, 7)
STATE_AT = (2, 4, 4, 6, 6, 7, 7, 8)
LOG2E = 1.4426950408889634


def dot(a, b):
    return jnp.dot(a, b, preferred_element_type=F32)


def dot_nt(a, b):
    return lax.dot_general(a, b, (((1,), (1,)), ((), ())), preferred_element_type=F32)


def dot_tn(a, b):
    return lax.dot_general(a, b, (((0,), (0,)), ((), ())), preferred_element_type=F32)


def split3(a):
    hi = a.astype(BF16)
    rest = a - hi.astype(F32)
    mid = rest.astype(BF16)
    low = (rest - mid.astype(F32)).astype(BF16)
    return hi, mid, low


def kernel(
    x_hbm, g_hbm, b_hbm, c_hbm, ld_hbm, tab_hbm, resets_ref, ids_ref, skip_ref,
    out, proj_out,
    x, g, cb, cbt, ld, tab, logs, cbm, vis, paired, onehot, wcat, spread,
    u, gi, wts, loc, acc, sa, own_d, partner_sa, partner_d,
    tot, tot_d, yin, yin_d, ypre, gt, gd, xin, xin_d, xpre, rt, rd, zin, zin_d,
    xo, gc, yo, w, full,
    lsem, hs, hr, ps, pr, pds, pdr, y1s, y1r, yds, ydr, x1s, x1r, xds, xdr, z1s, z1r, zds, zdr,
    x2s, x2r, y2s, y2r, p2s, p2r, ready, ld_own,
):
    cx = lax.axis_index("ctx")
    hd = lax.axis_index("head")
    zz, xx = cx // 4, cx % 4
    yy, core = hd // 2, hd % 2
    mydir = 1 - core
    pos_y = core * yy + (1 - core) * (3 - yy)
    pos_x = core * xx + (1 - core) * (3 - xx)
    pos_z = core * zz + (1 - core) * (7 - zz)

    def at4(q):
        return core * q + (1 - core) * (3 - q)

    def at8(q):
        return core * q + (1 - core) * (7 - q)

    def remote(src, dst, s, r, dev):
        return pltpu.make_async_remote_copy(
            src_ref=src, dst_ref=dst, send_sem=s, recv_sem=r, device_id=dev, device_id_type=MESH
        )

    def half(i):
        return pl.ds(i * HALF, HALF)

    def piece(i, place):
        return pl.ds(pl.multiple_of(i * HALF + place * PIECE, PIECE), PIECE)

    ld[:, 6:8, :] = jnp.zeros((8, 2, TOK), F32)
    zin_d[...] = jnp.zeros_like(zin_d)
    zin[...] = jnp.zeros_like(zin)

    barrier = pltpu.get_barrier_semaphore()
    for k in (2, 6, 1, 7):
        pl.semaphore_signal(barrier, inc=1, device_id=(((zz + k) % 8) * 4 + xx, hd), device_id_type=MESH)
    for k in range(1, 8):
        pl.semaphore_signal(barrier, inc=1, device_id=(cx, (hd + k) % 8), device_id_type=MESH)
    for k in range(1, 4):
        pl.semaphore_signal(barrier, inc=1, device_id=(zz * 4 + (xx + k) % 4, hd), device_id_type=MESH)

    mine = pl.ds(pl.multiple_of(hd * TOK, TOK), TOK)
    own_ld = pltpu.make_async_copy(ld_hbm, ld_own, lsem.at[5])
    loads = [
        pltpu.make_async_copy(g_hbm, g, lsem.at[0]),
        pltpu.make_async_copy(b_hbm.at[mine, :], cb.at[1], lsem.at[1]),
        pltpu.make_async_copy(c_hbm.at[mine, :], cb.at[0], lsem.at[2]),
        pltpu.make_async_copy(x_hbm, x, lsem.at[3]),
    ]
    own_tab = pltpu.make_async_copy(tab_hbm, tab.at[hd], lsem.at[4])
    own_ld.start()
    own_tab.start()
    for one in (loads[1], loads[2], loads[0], loads[3]):
        one.start()

    own_ld.wait()
    pl.semaphore_wait(barrier, 14)

    def ld_copy(k):
        to = (hd + k) % 8
        theirs = pl.ds(pl.multiple_of(to * TOK, TOK), TOK)
        return remote(
            ld_own.at[:, theirs], ld.at[hd, pl.ds(0, 6), :], hs.at[0, k - 1], hr.at[0, k - 1], (cx, to)
        )

    def tab_copy(k):
        return remote(tab.at[hd], tab.at[hd], hs.at[1, k - 1], hr.at[1, k - 1], (cx, (hd + k) % 8))

    for k in (4, 3, 5, 2, 6, 1, 7):
        ld_copy(k).start()
    own_tab.wait()
    for k in (4, 3, 5, 2, 6, 1, 7):
        tab_copy(k).start()
    for k in (2, 6):
        pl.semaphore_signal(ready, inc=1, device_id=(((zz + k) % 8) * 4 + xx, hd), device_id_type=MESH)
    ld[hd, 0:6, :] = ld_own[:, mine]

    paired[...] = jnp.zeros_like(paired)

    def build(j, carry):
        r3 = lax.broadcasted_iota(jnp.int32, (192, GROUP), 0)
        c3 = lax.broadcasted_iota(jnp.int32, (192, GROUP), 1)
        spread[:, pl.ds(pl.multiple_of(j * GROUP, 128), GROUP)] = (
            ((r3 & 63) == 8 * j + (c3 >> 6)).astype(F32).astype(BF16)
        )
        return carry

    lax.fori_loop(0, 8, build, 0)
    row = lax.broadcasted_iota(jnp.int32, (TOK, TOK), 0)
    col = lax.broadcasted_iota(jnp.int32, (TOK, TOK), 1)
    upper = (row <= col).astype(F32).astype(BF16)
    flags = resets_ref[:, mine].astype(F32)
    seen = dot(jnp.broadcast_to(flags, (8, TOK)).astype(BF16), upper)
    seen_row = seen[0:1, :]
    seen_col = jnp.transpose(seen)[:, 0:1]
    visible = ((col <= row) & (seen_row == seen_col)).astype(F32)
    vis[...] = visible
    loads[1].wait()
    loads[2].wait()
    cbm[...] = dot_nt(cb[0], cb[1]) * visible
    cbt[0] = jnp.transpose(cb[0].astype(F32)).astype(BF16)
    cbt[1] = jnp.transpose(cb[1].astype(F32)).astype(BF16)
    agent = lax.broadcasted_iota(jnp.int32, (64, TOK), 0)
    picked = (agent == ids_ref[:, mine]).astype(F32)
    onehot[...] = jnp.transpose(picked).astype(BF16)

    for k in range(1, 8):
        ld_copy(k).wait_recv()
    hi, mid, low = split3(ld[...].reshape(64, TOK))
    run = (dot(hi, upper) + dot(mid, upper) + dot(low, upper)) * LOG2E
    logs[...] = run.reshape(8, 8, TOK)
    run_end = run[:, TOK - 1 : TOK]
    seen_end = seen_row[:, TOK - 1 : TOK]
    start = jnp.where(seen_row == 0, jnp.exp2(run), 0.0)
    end = jnp.where(seen_row == seen_end, jnp.exp2(jnp.minimum(run_end - run, 0.0)), 0.0)
    for index, value in ((0, start), (1, end)):
        turned = jnp.transpose(value)
        wcat[index] = jnp.concatenate(split3(turned), axis=1)

    loads[0].wait()

    def columns(j):
        return pl.ds(pl.multiple_of(j * GROUP, 128), GROUP)

    partner = (cx, yy * 2 + 1 - core)

    def p0(j):
        return remote(sa.at[core, j], partner_sa.at[j], ps.at[j], pr.at[j], partner)

    def p0_d():
        return remote(own_d, partner_d, pds.at[0], pdr.at[0], partner)

    def slice_columns(j):
        return pl.ds(pl.multiple_of(j * SLICE, 128), SLICE)

    def prepare_adjoint(j, carry):
        cols = slice_columns(j)
        weight = dot(wcat[0], spread[:, cols])
        own_d[:, cols] = weight[TOK - 1 : TOK, :]
        starts = (weight * g[:, cols].astype(F32)).astype(BF16)
        sa[1, j] = dot(cbt[0], starts).astype(BF16)

        @pl.when(core == 1)
        def _():
            p0(j).start()

        return carry

    lax.fori_loop(0, 4, prepare_adjoint, 0)

    p0_d().start()

    loads[3].wait()
    for k in range(1, 8):
        tab_copy(k).wait_recv()

    def y1(i, k):
        to = at4((pos_y + k) % 4)
        return remote(
            tot.at[to, half(i), :], yin.at[pos_y, half(i), :], y1s.at[i, k - 1], y1r.at[i, k - 1], (cx, to * 2 + core)
        )

    def y1_d(k):
        to = at4((pos_y + k) % 4)
        return remote(tot_d.at[to], yin_d.at[pos_y], yds.at[k - 1], ydr.at[k - 1], (cx, to * 2 + core))

    def x1(i, k):
        to = at4((pos_x + k) % 4)
        return remote(
            gt.at[piece(i, to), :], xin.at[i, pos_x], x1s.at[i, k - 1], x1r.at[i, k - 1], (zz * 4 + to, hd)
        )

    def x1_d(k):
        to = at4((pos_x + k) % 4)
        return remote(gd, xin_d.at[pos_x], xds.at[k - 1], xdr.at[k - 1], (zz * 4 + to, hd))

    def z1(i, k):
        to = at8((pos_z + k) % 8)
        return remote(rt.at[i], zin.at[i, k - 1], z1s.at[i, k - 1], z1r.at[i, k - 1], (to * 4 + xx, hd))

    def z1_d(k):
        to = at8((pos_z + k) % 8)
        return remote(rd, zin_d.at[k - 1], zds.at[k - 1], zdr.at[k - 1], (to * 4 + xx, hd))

    def x2(i, k):
        to = (pos_x + k) % 4
        return remote(
            xo.at[i, to], gc.at[piece(i, xx), :], x2s.at[i, k - 1], x2r.at[i, k - 1], (zz * 4 + at4(to), hd)
        )

    def y2(i, k):
        to = (pos_y + k) % 4
        return remote(
            yo.at[to, half(i), :], w.at[yy, half(i), :], y2s.at[i, k - 1], y2r.at[i, k - 1], (cx, at4(to) * 2 + core)
        )

    def came(k):
        return at4((pos_y - k + 4) % 4)

    def p2(i, k):
        j = came(k)
        return remote(w.at[j, half(i), :], full.at[mydir, j, half(i), :], p2s.at[i, k], p2r.at[i, k], partner)

    def total(i):
        if i == 0:
            p0_d().wait_recv()
            for k in (2, 1, 3, 0):
                to = at4((pos_y + k) % 4)
                at = pl.ds(pl.multiple_of(to * SLICE, 128), SLICE)
                both = own_d[:, at] * partner_d[:, at]
                if k:
                    tot_d[to] = both
                    y1_d(k).start()
                else:
                    yin_d[pos_y] = both
        for k in (2, 1, 3, 0):
            to = at4((pos_y + k) % 4)
            at = pl.ds(pl.multiple_of(to * SLICE, 128), SLICE)
            d = own_d[:, at]
            if i == 0:
                p0(to).wait_recv()
            value = (
                d * partner_sa[to, half(i), :].astype(F32) + sa[mydir, to, half(i), :].astype(F32)
            ).astype(BF16)
            if k:
                tot[to, half(i), :] = value
                y1(i, k).start()
            else:
                yin[pos_y, half(i), :] = value

    def group_y(i):
        if i == 0:
            for k in (1, 3, 2):
                y1_d(k).wait_recv()
            gd[...] = yin_d[0] * yin_d[1] * yin_d[2] * yin_d[3]
            for k in (2, 1, 3):
                x1_d(k).start()
            xin_d[pos_x] = gd[...]
        for k in (1, 3, 2):
            y1(i, k).wait_recv()

        def chunk(n, carry):
            rows = piece(i, n)
            held = yin[0, rows, :].astype(F32)
            for p in range(1, 4):
                ypre[p - 1, rows, :] = held
                held = yin_d[p] * held + yin[p, rows, :].astype(F32)
            gt[rows, :] = held.astype(BF16)
            return carry

        lax.fori_loop(0, 4, chunk, 0)
        for k in (2, 1, 3):
            x1(i, k).start()
        xin[i, pos_x] = gt[piece(i, xx), :]

    def group_x(i):
        if i == 0:
            for k in (1, 3, 2):
                x1_d(k).wait_recv()
            rd[...] = xin_d[0] * xin_d[1] * xin_d[2] * xin_d[3]
            pl.semaphore_wait(ready, 2)
            for k in (4, 3, 5, 2, 6, 1, 7):

                @pl.when(pos_z + k < 8)
                def _():
                    z1_d(k).start()

        for k in (1, 3, 2):
            x1(i, k).wait_recv()
        held = xin[i, 0].astype(F32)
        for p in range(1, 4):
            xpre[i, p - 1] = held
            held = xin_d[p] * held + xin[i, p].astype(F32)
        rt[i] = held.astype(BF16)
        for k in (4, 3, 5, 2, 6, 1, 7):

            @pl.when(pos_z + k < 8)
            def _():
                z1(i, k).start()

    def back_x(i):
        for k in range(1, 8):

            @pl.when(pos_z >= k)
            def _():
                z1(i, k).wait_recv()
                if i == 0:
                    z1_d(k).wait_recv()

        held = zin[i, 0].astype(F32)
        weight = zin_d[0]
        for k in range(1, 7):
            held = held + weight * zin[i, k].astype(F32)
            weight = weight * zin_d[k]
        xo[i, 0] = held.astype(BF16)
        prod = xin_d[0]
        for p in range(1, 4):
            xo[i, p] = (prod * held + xpre[i, p - 1]).astype(BF16)
            prod = prod * xin_d[p]
        for k in (2, 1, 3):
            x2(i, k).start()
        gc[piece(i, xx), :] = xo[i, pos_x]

    def back_y(i):
        for k in (1, 3, 2):
            x2(i, k).wait_recv()

        def chunk(n, carry):
            rows = piece(i, n)
            base = gc[rows, :].astype(F32)
            yo[0, rows, :] = gc[rows, :]
            prod = yin_d[0]
            for p in range(1, 4):
                yo[p, rows, :] = (prod * base + ypre[p - 1, rows, :]).astype(BF16)
                prod = prod * yin_d[p]
            return carry

        lax.fori_loop(0, 4, chunk, 0)
        for k in (2, 1, 3):
            y2(i, k).start()
        w[yy, half(i), :] = yo[pos_y, half(i), :]

    def forward(i):
        for k in (0, 1, 3, 2):
            if k:
                y2(i, k).wait_recv()
            p2(i, k).start()

    def own_carry(i, k):
        j = came(k)
        at = pl.ds(pl.multiple_of(j * SLICE, 128), SLICE)
        full[mydir, j, half(i), :] = (
            partner_d[:, at] * w[j, half(i), :].astype(F32) + partner_sa[j, half(i), :].astype(F32)
        ).astype(BF16)

    def finish(way, j):
        at = pl.ds(pl.multiple_of(j * SLICE, 128), SLICE)
        carried = full[way, j]
        out[way, :, at] = (loc[way, :, at] + wts[way, :, at] * dot(cb[way], carried)).astype(BF16)
        acc[way] += dot_nt(gi[way, :, at], carried)

    @pl.when(core == 0)
    def _():
        total(0)
        total(1)

    def prepare_state(turn, carry):
        step = jnp.where(turn == 0, 2, jnp.where(turn == 1, 1, jnp.where(turn == 2, 3, 0)))
        j = (yy + step) % 4
        cols = slice_columns(j)
        rows = jnp.concatenate([tab[j * 2], tab[j * 2 + 1]], axis=1)
        inputs = (x[:, cols].astype(F32) + dot(onehot[...], rows)).astype(BF16)
        u[:, cols] = inputs
        ends = (dot(wcat[1], spread[:, cols]) * inputs.astype(F32)).astype(BF16)
        sa[0, j] = dot(cbt[1], ends).astype(BF16)

        @pl.when(core == 0)
        def _():
            p0(j).start()

        return carry

    lax.fori_loop(0, 4, prepare_state, 0)

    @pl.when(core == 1)
    def _():
        total(0)
        total(1)

    lane = lax.broadcasted_iota(jnp.int32, (TOK, 128), 1)
    first = lane < 64

    def intra(j, carry):
        for adjoint_at, state_at, act, part in (
            (ADJOINT_AT[0], STATE_AT[0], group_y, 0),
            (ADJOINT_AT[1], STATE_AT[1], group_x, 0),
            (ADJOINT_AT[2], STATE_AT[2], group_y, 1),
            (ADJOINT_AT[3], STATE_AT[3], group_x, 1),
            (ADJOINT_AT[4], STATE_AT[4], back_x, 0),
            (ADJOINT_AT[5], STATE_AT[5], back_x, 1),
            (ADJOINT_AT[6], STATE_AT[6], back_y, 0),
            (ADJOINT_AT[7], STATE_AT[7], back_y, 1),
        ):
            pl.when(j == core * state_at + mydir * adjoint_at)(functools.partial(act, part))
        pl.when(j < 8)(functools.partial(local, j))
        return carry

    def local(j):
        rows_l = logs[j]
        cols_l = jnp.transpose(rows_l)
        wide = columns(j)
        for way, values in ((0, g), (1, u)):
            weight = dot(wcat[way], spread[:, wide])
            wts[way, :, wide] = weight
            gi[way, :, wide] = (weight * values[:, wide].astype(F32)).astype(BF16)
        for pair in range(3):
            cols = pl.ds(pl.multiple_of(j * GROUP + pair * 128, 128), 128)
            up = u[:, cols]
            gp = g[:, cols]
            zero = jnp.zeros_like(gp)
            ys, dus = [], []
            for side in range(2):
                r = pair * 2 + side
                lr = rows_l[r : r + 1, :]
                lc = cols_l[:, r : r + 1]
                gm = jnp.where(first, gp, zero) if side == 0 else jnp.where(first, zero, gp)
                da = jnp.exp2(jnp.minimum(lc[:128] - lr[:, :128], 0.0))
                mix_a = (da * cbm[:128, :128]).astype(BF16)
                paired[:128, :128] += da * dot_nt(gm[:128], up[:128])
                db = jnp.exp2(jnp.minimum(lc[128:] - lr, 0.0))
                mix_b = (db * cbm[128:, :]).astype(BF16)
                paired[128:, :] += db * dot_nt(gm[128:], up)
                ys.append((dot(mix_a, up[:128]), dot(mix_b, up)))
                low = dot_tn(mix_b, gp[128:])
                dus.append((low[:128] + dot_tn(mix_a, gp[:128]), low[128:]))
            s0 = skip_ref[j * 6 + pair * 2]
            s1 = skip_ref[j * 6 + pair * 2 + 1]
            scale = jnp.where(first[:128], s0, s1)
            for part in range(2):
                at = slice(part * 128, part * 128 + 128)
                loc[0, at, cols] = jnp.where(first[at], ys[0][part], ys[1][part]) + scale * up[at].astype(F32)
                loc[1, at, cols] = jnp.where(first[at], dus[0][part], dus[1][part]) + scale * gp[at].astype(F32)

    lax.fori_loop(0, 9, intra, 0)

    pairs = (paired[...] * vis[...]).astype(BF16)
    acc[0] = dot(pairs, cb[1])
    acc[1] = dot_tn(pairs, cb[0])

    def carried_here(way):
        forward(0)
        for k in range(4):
            own_carry(0, k)
        forward(1)
        for k in (0, 1, 3, 2):
            own_carry(1, k)
            finish(way, came(k))

    def carried_there(way):
        for k in (0, 1, 3, 2):
            p2(0, k).wait_recv()
            p2(1, k).wait_recv()
            finish(way, at4((pos_y + k) % 4))

    @pl.when(core == 0)
    def _():
        carried_here(1)
        carried_there(0)

    @pl.when(core == 1)
    def _():
        carried_there(1)
        carried_here(0)

    proj_out[...] = acc[...].astype(BF16)

    for k in range(1, 8):
        ld_copy(k).wait_send()
        tab_copy(k).wait_send()

        @pl.when(pos_z + k < 8)
        def _():
            z1_d(k).wait_send()
            for i in range(CHUNKS):
                z1(i, k).wait_send()

    p0_d().wait_send()
    for k in range(1, 4):
        y1_d(k).wait_send()
        x1_d(k).wait_send()
    for j in range(4):
        p0(j).wait_send()
    for i in range(CHUNKS):
        for k in range(1, 4):
            for make in (y1, x1, x2, y2):
                make(i, k).wait_send()
        for k in range(4):
            p2(i, k).wait_send()


def store_kernel(values, proj, y_out, du_out, db_out, dc_out, sem):
    moves = [(proj.at[1], db_out), (proj.at[0], dc_out)]
    for part in range(4):
        rows = pl.ds(part * 64, 64)
        moves += [(values.at[0, rows], y_out.at[rows]), (values.at[1, rows], du_out.at[rows])]
    copies = [pltpu.make_async_copy(src, dst, sem.at[i]) for i, (src, dst) in enumerate(moves)]
    for one in copies:
        one.start()
    for one in copies:
        one.wait()


def body(layer_input, cotangent, b_proj, c_proj, log_decay, resets, agent_ids, skip_gain, agent_table):
    dma = pltpu.SemaphoreType.DMA
    vm = pltpu.VMEM
    any_spec = pl.BlockSpec(memory_space=pl.ANY)
    vmem_spec = pl.BlockSpec(memory_space=pltpu.VMEM)
    wide = (TOK, FEAT)
    n = CHUNKS
    hbm = [
        pltpu.with_memory_space_constraint(a, pltpu.HBM)
        for a in (layer_input, cotangent, b_proj, c_proj, log_decay.T, agent_table)
    ]
    values, proj = pl.pallas_call(
        kernel,
        out_shape=(vm((2, TOK, FEAT), BF16), vm((2, TOK, STATE), BF16)),
        in_specs=[any_spec] * 6 + [vmem_spec] * 2 + [pl.BlockSpec(memory_space=pltpu.SMEM)],
        out_specs=(vmem_spec, vmem_spec),
        scratch_shapes=[
            vm(wide, BF16), vm(wide, BF16), vm((2, TOK, STATE), BF16), vm((2, STATE, TOK), BF16),
            vm((8, 8, TOK), F32), vm((8, 64, GROUP), BF16), vm((8, 8, TOK), F32),
            vm((TOK, TOK), F32), vm((TOK, TOK), F32), vm((TOK, TOK), F32),
            vm((TOK, 64), BF16), vm((2, TOK, 192), BF16), vm((192, FEAT), BF16),
            vm(wide, BF16), vm((2, TOK, FEAT), BF16), vm((2, TOK, FEAT), F32), vm((2, TOK, FEAT), F32),
            vm((2, TOK, STATE), F32),
            vm((2, 4, STATE, SLICE), BF16), vm((1, FEAT), F32), vm((4, STATE, SLICE), BF16), vm((1, FEAT), F32),
            vm((4, STATE, SLICE), BF16), vm((4, 1, SLICE), F32),
            vm((4, STATE, SLICE), BF16), vm((4, 1, SLICE), F32), vm((3, STATE, SLICE), F32),
            vm((STATE, SLICE), BF16), vm((1, SLICE), F32),
            vm((n, 4, PIECE, SLICE), BF16), vm((4, 1, SLICE), F32), vm((n, 3, PIECE, SLICE), F32),
            vm((n, PIECE, SLICE), BF16), vm((1, SLICE), F32),
            vm((n, 7, PIECE, SLICE), BF16), vm((7, 1, SLICE), F32),
            vm((n, 4, PIECE, SLICE), BF16), vm((STATE, SLICE), BF16),
            vm((4, STATE, SLICE), BF16), vm((4, STATE, SLICE), BF16), vm((2, 4, STATE, SLICE), BF16),
            dma((6,)), dma((2, 7)), dma((2, 7)), dma((4,)), dma((4,)), dma((1,)), dma((1,)),
            dma((n, 3)), dma((n, 3)), dma((3,)), dma((3,)),
            dma((n, 3)), dma((n, 3)), dma((3,)), dma((3,)),
            dma((n, 7)), dma((n, 7)), dma((7,)), dma((7,)),
            dma((n, 3)), dma((n, 3)), dma((n, 3)), dma((n, 3)), dma((n, 4)), dma((n, 4)),
            pltpu.SemaphoreType.REGULAR, vm((6, 8 * TOK), F32),
        ],
        compiler_params=pltpu.CompilerParams(
            collective_id=0, has_side_effects=True, vmem_limit_bytes=56 * 1024 * 1024
        ),
        name="tract_scan",
    )(*hbm, resets.reshape(1, -1), agent_ids.reshape(1, -1), skip_gain)
    token = jax.ShapeDtypeStruct(wide, BF16)
    narrow = jax.ShapeDtypeStruct((TOK, STATE), BF16)
    return pl.pallas_call(
        store_kernel,
        out_shape=(token, token, narrow, narrow),
        in_specs=[any_spec] * 2,
        out_specs=(any_spec,) * 4,
        scratch_shapes=[dma((10,))],
        name="store",
    )(pltpu.with_memory_space_constraint(values, vm), pltpu.with_memory_space_constraint(proj, vm))


def solution(mesh):
    return jax.shard_map(
        body,
        mesh=mesh,
        in_specs=(
            P(("ctx", "head"), None),
            P(("ctx", "head"), None),
            P("ctx", None),
            P("ctx", None),
            P("ctx", "head"),
            P("ctx"),
            P("ctx"),
            P(),
            P(None, "head"),
        ),
        out_specs=(P(("ctx", "head"), None),) * 4,
        check_vma=False,
    )
```

```python
import functools

import jax
import jax.numpy as jnp
from jax import lax
from jax.experimental import pallas as pl
from jax.experimental.pallas import tpu as pltpu
from jax.sharding import PartitionSpec as P

MESH = pl.DeviceIdType.MESH
F32 = jnp.float32
BF16 = jnp.bfloat16
TOK = 256
FEAT = 3072
STATE = 128
GROUP = 384
SLICE = 768
HALF = 64
PIECE = 16
CHUNKS = 2
ADJOINT_AT = (1, 3, 2, 5, 5, 6, 6, 7)
STATE_AT = (2, 4, 4, 6, 6, 7, 7, 8)
LOG2E = 1.4426950408889634


def dot(a, b):
    return jnp.dot(a, b, preferred_element_type=F32)


def dot_nt(a, b):
    return lax.dot_general(a, b, (((1,), (1,)), ((), ())), preferred_element_type=F32)


def dot_tn(a, b):
    return lax.dot_general(a, b, (((0,), (0,)), ((), ())), preferred_element_type=F32)


def split3(a):
    hi = a.astype(BF16)
    rest = a - hi.astype(F32)
    mid = rest.astype(BF16)
    low = (rest - mid.astype(F32)).astype(BF16)
    return hi, mid, low


def kernel(
    x_hbm, g_hbm, b_hbm, c_hbm, ld_hbm, tab_hbm, resets_hbm, ids_hbm, skip_hbm,
    out, proj_out,
    x, g, cb, cbt, ld, tab, logs, cbm, vis, paired, onehot, wcat, spread,
    u, gi, wts, loc, acc, sa, own_d, partner_sa, partner_d,
    tot, tot_d, yin, yin_d, ypre, gt, gd, xin, xin_d, xpre, rt, rd, zin, zin_d,
    xo, gc, yo, w, full,
    lsem, hs, hr, ps, pr, pds, pdr, y1s, y1r, yds, ydr, x1s, x1r, xds, xdr, z1s, z1r, zds, zdr,
    x2s, x2r, y2s, y2r, p2s, p2r, ready, ld_own, resets_ref, ids_ref, skip_ref,
):
    cx = lax.axis_index("ctx")
    hd = lax.axis_index("head")
    zz, xx = cx // 4, cx % 4
    yy, core = hd // 2, hd % 2
    mydir = 1 - core
    pos_y = core * yy + (1 - core) * (3 - yy)
    pos_x = core * xx + (1 - core) * (3 - xx)
    pos_z = core * zz + (1 - core) * (7 - zz)

    def at4(q):
        return core * q + (1 - core) * (3 - q)

    def at8(q):
        return core * q + (1 - core) * (7 - q)

    def remote(src, dst, s, r, dev):
        return pltpu.make_async_remote_copy(
            src_ref=src, dst_ref=dst, send_sem=s, recv_sem=r, device_id=dev, device_id_type=MESH
        )

    def half(i):
        return pl.ds(i * HALF, HALF)

    def piece(i, place):
        return pl.ds(pl.multiple_of(i * HALF + place * PIECE, PIECE), PIECE)

    ld[:, 6:8, :] = jnp.zeros((8, 2, TOK), F32)
    zin_d[...] = jnp.zeros_like(zin_d)
    zin[...] = jnp.zeros_like(zin)

    barrier = pltpu.get_barrier_semaphore()
    for k in (2, 6, 1, 7):
        pl.semaphore_signal(barrier, inc=1, device_id=(((zz + k) % 8) * 4 + xx, hd), device_id_type=MESH)
    for k in range(1, 8):
        pl.semaphore_signal(barrier, inc=1, device_id=(cx, (hd + k) % 8), device_id_type=MESH)
    for k in range(1, 4):
        pl.semaphore_signal(barrier, inc=1, device_id=(zz * 4 + (xx + k) % 4, hd), device_id_type=MESH)

    mine = pl.ds(pl.multiple_of(hd * TOK, TOK), TOK)
    own_ld = pltpu.make_async_copy(ld_hbm, ld_own, lsem.at[5])
    loads = [
        pltpu.make_async_copy(g_hbm, g, lsem.at[0]),
        pltpu.make_async_copy(b_hbm.at[mine, :], cb.at[1], lsem.at[1]),
        pltpu.make_async_copy(c_hbm.at[mine, :], cb.at[0], lsem.at[2]),
        pltpu.make_async_copy(x_hbm, x, lsem.at[3]),
    ]
    own_tab = pltpu.make_async_copy(tab_hbm, tab.at[hd], lsem.at[4])
    small = [
        pltpu.make_async_copy(resets_hbm, resets_ref, lsem.at[6]),
        pltpu.make_async_copy(ids_hbm, ids_ref, lsem.at[7]),
        pltpu.make_async_copy(skip_hbm, skip_ref, lsem.at[8]),
    ]
    own_ld.start()
    own_tab.start()
    for one in small:
        one.start()
    for one in (loads[1], loads[2], loads[0], loads[3]):
        one.start()

    own_ld.wait()
    pl.semaphore_wait(barrier, 14)

    def ld_copy(k):
        to = (hd + k) % 8
        theirs = pl.ds(pl.multiple_of(to * TOK, TOK), TOK)
        return remote(
            ld_own.at[:, theirs], ld.at[hd, pl.ds(0, 6), :], hs.at[0, k - 1], hr.at[0, k - 1], (cx, to)
        )

    def tab_copy(k):
        return remote(tab.at[hd], tab.at[hd], hs.at[1, k - 1], hr.at[1, k - 1], (cx, (hd + k) % 8))

    for k in (4, 3, 5, 2, 6, 1, 7):
        ld_copy(k).start()
    own_tab.wait()
    for k in (4, 3, 5, 2, 6, 1, 7):
        tab_copy(k).start()
    for k in (2, 6):
        pl.semaphore_signal(ready, inc=1, device_id=(((zz + k) % 8) * 4 + xx, hd), device_id_type=MESH)
    ld[hd, 0:6, :] = ld_own[:, mine]

    paired[...] = jnp.zeros_like(paired)

    def build(j, carry):
        r3 = lax.broadcasted_iota(jnp.int32, (192, GROUP), 0)
        c3 = lax.broadcasted_iota(jnp.int32, (192, GROUP), 1)
        spread[:, pl.ds(pl.multiple_of(j * GROUP, 128), GROUP)] = (
            ((r3 & 63) == 8 * j + (c3 >> 6)).astype(F32).astype(BF16)
        )
        return carry

    lax.fori_loop(0, 8, build, 0)
    row = lax.broadcasted_iota(jnp.int32, (TOK, TOK), 0)
    col = lax.broadcasted_iota(jnp.int32, (TOK, TOK), 1)
    upper = (row <= col).astype(F32).astype(BF16)
    for one in small:
        one.wait()
    flags = resets_ref[:, mine].astype(F32)
    seen = dot(jnp.broadcast_to(flags, (8, TOK)).astype(BF16), upper)
    seen_row = seen[0:1, :]
    seen_col = jnp.transpose(seen)[:, 0:1]
    visible = ((col <= row) & (seen_row == seen_col)).astype(F32)
    vis[...] = visible
    loads[1].wait()
    loads[2].wait()
    cbm[...] = dot_nt(cb[0], cb[1]) * visible
    cbt[0] = jnp.transpose(cb[0].astype(F32)).astype(BF16)
    cbt[1] = jnp.transpose(cb[1].astype(F32)).astype(BF16)
    agent = lax.broadcasted_iota(jnp.int32, (64, TOK), 0)
    picked = (agent == ids_ref[:, mine]).astype(F32)
    onehot[...] = jnp.transpose(picked).astype(BF16)

    for k in range(1, 8):
        ld_copy(k).wait_recv()
    hi, mid, low = split3(ld[...].reshape(64, TOK))
    run = (dot(hi, upper) + dot(mid, upper) + dot(low, upper)) * LOG2E
    logs[...] = run.reshape(8, 8, TOK)
    run_end = run[:, TOK - 1 : TOK]
    seen_end = seen_row[:, TOK - 1 : TOK]
    start = jnp.where(seen_row == 0, jnp.exp2(run), 0.0)
    end = jnp.where(seen_row == seen_end, jnp.exp2(jnp.minimum(run_end - run, 0.0)), 0.0)
    for index, value in ((0, start), (1, end)):
        turned = jnp.transpose(value)
        wcat[index] = jnp.concatenate(split3(turned), axis=1)

    loads[0].wait()

    def columns(j):
        return pl.ds(pl.multiple_of(j * GROUP, 128), GROUP)

    partner = (cx, yy * 2 + 1 - core)

    def p0(j):
        return remote(sa.at[core, j], partner_sa.at[j], ps.at[j], pr.at[j], partner)

    def p0_d():
        return remote(own_d, partner_d, pds.at[0], pdr.at[0], partner)

    def slice_columns(j):
        return pl.ds(pl.multiple_of(j * SLICE, 128), SLICE)

    def prepare_adjoint(j, carry):
        cols = slice_columns(j)
        weight = dot(wcat[0], spread[:, cols])
        own_d[:, cols] = weight[TOK - 1 : TOK, :]
        starts = (weight * g[:, cols].astype(F32)).astype(BF16)
        sa[1, j] = dot(cbt[0], starts).astype(BF16)

        @pl.when(core == 1)
        def _():
            p0(j).start()

        return carry

    lax.fori_loop(0, 4, prepare_adjoint, 0)

    p0_d().start()

    loads[3].wait()
    for k in range(1, 8):
        tab_copy(k).wait_recv()

    def y1(i, k):
        to = at4((pos_y + k) % 4)
        return remote(
            tot.at[to, half(i), :], yin.at[pos_y, half(i), :], y1s.at[i, k - 1], y1r.at[i, k - 1], (cx, to * 2 + core)
        )

    def y1_d(k):
        to = at4((pos_y + k) % 4)
        return remote(tot_d.at[to], yin_d.at[pos_y], yds.at[k - 1], ydr.at[k - 1], (cx, to * 2 + core))

    def x1(i, k):
        to = at4((pos_x + k) % 4)
        return remote(
            gt.at[piece(i, to), :], xin.at[i, pos_x], x1s.at[i, k - 1], x1r.at[i, k - 1], (zz * 4 + to, hd)
        )

    def x1_d(k):
        to = at4((pos_x + k) % 4)
        return remote(gd, xin_d.at[pos_x], xds.at[k - 1], xdr.at[k - 1], (zz * 4 + to, hd))

    def z1(i, k):
        to = at8((pos_z + k) % 8)
        return remote(rt.at[i], zin.at[i, k - 1], z1s.at[i, k - 1], z1r.at[i, k - 1], (to * 4 + xx, hd))

    def z1_d(k):
        to = at8((pos_z + k) % 8)
        return remote(rd, zin_d.at[k - 1], zds.at[k - 1], zdr.at[k - 1], (to * 4 + xx, hd))

    def x2(i, k):
        to = (pos_x + k) % 4
        return remote(
            xo.at[i, to], gc.at[piece(i, xx), :], x2s.at[i, k - 1], x2r.at[i, k - 1], (zz * 4 + at4(to), hd)
        )

    def y2(i, k):
        to = (pos_y + k) % 4
        return remote(
            yo.at[to, half(i), :], w.at[yy, half(i), :], y2s.at[i, k - 1], y2r.at[i, k - 1], (cx, at4(to) * 2 + core)
        )

    def came(k):
        return at4((pos_y - k + 4) % 4)

    def p2(i, k):
        j = came(k)
        return remote(w.at[j, half(i), :], full.at[mydir, j, half(i), :], p2s.at[i, k], p2r.at[i, k], partner)

    def total(i):
        if i == 0:
            p0_d().wait_recv()
            for k in (2, 1, 3, 0):
                to = at4((pos_y + k) % 4)
                at = pl.ds(pl.multiple_of(to * SLICE, 128), SLICE)
                both = own_d[:, at] * partner_d[:, at]
                if k:
                    tot_d[to] = both
                    y1_d(k).start()
                else:
                    yin_d[pos_y] = both
        for k in (2, 1, 3, 0):
            to = at4((pos_y + k) % 4)
            at = pl.ds(pl.multiple_of(to * SLICE, 128), SLICE)
            d = own_d[:, at]
            if i == 0:
                p0(to).wait_recv()
            value = (
                d * partner_sa[to, half(i), :].astype(F32) + sa[mydir, to, half(i), :].astype(F32)
            ).astype(BF16)
            if k:
                tot[to, half(i), :] = value
                y1(i, k).start()
            else:
                yin[pos_y, half(i), :] = value

    def group_y(i):
        if i == 0:
            for k in (1, 3, 2):
                y1_d(k).wait_recv()
            gd[...] = yin_d[0] * yin_d[1] * yin_d[2] * yin_d[3]
            for k in (2, 1, 3):
                x1_d(k).start()
            xin_d[pos_x] = gd[...]
        for k in (1, 3, 2):
            y1(i, k).wait_recv()

        def chunk(n, carry):
            rows = piece(i, n)
            held = yin[0, rows, :].astype(F32)
            for p in range(1, 4):
                ypre[p - 1, rows, :] = held
                held = yin_d[p] * held + yin[p, rows, :].astype(F32)
            gt[rows, :] = held.astype(BF16)
            return carry

        lax.fori_loop(0, 4, chunk, 0)
        for k in (2, 1, 3):
            x1(i, k).start()
        xin[i, pos_x] = gt[piece(i, xx), :]

    def group_x(i):
        if i == 0:
            for k in (1, 3, 2):
                x1_d(k).wait_recv()
            rd[...] = xin_d[0] * xin_d[1] * xin_d[2] * xin_d[3]
            pl.semaphore_wait(ready, 2)
            for k in (4, 3, 5, 2, 6, 1, 7):

                @pl.when(pos_z + k < 8)
                def _():
                    z1_d(k).start()

        for k in (1, 3, 2):
            x1(i, k).wait_recv()
        held = xin[i, 0].astype(F32)
        for p in range(1, 4):
            xpre[i, p - 1] = held
            held = xin_d[p] * held + xin[i, p].astype(F32)
        rt[i] = held.astype(BF16)
        for k in (4, 3, 5, 2, 6, 1, 7):

            @pl.when(pos_z + k < 8)
            def _():
                z1(i, k).start()

    def back_x(i):
        for k in range(1, 8):

            @pl.when(pos_z >= k)
            def _():
                z1(i, k).wait_recv()
                if i == 0:
                    z1_d(k).wait_recv()

        held = zin[i, 0].astype(F32)
        weight = zin_d[0]
        for k in range(1, 7):
            held = held + weight * zin[i, k].astype(F32)
            weight = weight * zin_d[k]
        xo[i, 0] = held.astype(BF16)
        prod = xin_d[0]
        for p in range(1, 4):
            xo[i, p] = (prod * held + xpre[i, p - 1]).astype(BF16)
            prod = prod * xin_d[p]
        for k in (2, 1, 3):
            x2(i, k).start()
        gc[piece(i, xx), :] = xo[i, pos_x]

    def back_y(i):
        for k in (1, 3, 2):
            x2(i, k).wait_recv()

        def chunk(n, carry):
            rows = piece(i, n)
            base = gc[rows, :].astype(F32)
            yo[0, rows, :] = gc[rows, :]
            prod = yin_d[0]
            for p in range(1, 4):
                yo[p, rows, :] = (prod * base + ypre[p - 1, rows, :]).astype(BF16)
                prod = prod * yin_d[p]
            return carry

        lax.fori_loop(0, 4, chunk, 0)
        for k in (2, 1, 3):
            y2(i, k).start()
        w[yy, half(i), :] = yo[pos_y, half(i), :]

    def forward(i):
        for k in (0, 1, 3, 2):
            if k:
                y2(i, k).wait_recv()
            p2(i, k).start()

    def own_carry(i, k):
        j = came(k)
        at = pl.ds(pl.multiple_of(j * SLICE, 128), SLICE)
        full[mydir, j, half(i), :] = (
            partner_d[:, at] * w[j, half(i), :].astype(F32) + partner_sa[j, half(i), :].astype(F32)
        ).astype(BF16)

    def finish(way, j):
        at = pl.ds(pl.multiple_of(j * SLICE, 128), SLICE)
        carried = full[way, j]
        out[way, :, at] = (loc[way, :, at] + wts[way, :, at] * dot(cb[way], carried)).astype(BF16)
        acc[way] += dot_nt(gi[way, :, at], carried)

    @pl.when(core == 0)
    def _():
        total(0)
        total(1)

    def prepare_state(turn, carry):
        step = jnp.where(turn == 0, 2, jnp.where(turn == 1, 1, jnp.where(turn == 2, 3, 0)))
        j = (yy + step) % 4
        cols = slice_columns(j)
        rows = jnp.concatenate([tab[j * 2], tab[j * 2 + 1]], axis=1)
        inputs = (x[:, cols].astype(F32) + dot(onehot[...], rows)).astype(BF16)
        u[:, cols] = inputs
        ends = (dot(wcat[1], spread[:, cols]) * inputs.astype(F32)).astype(BF16)
        sa[0, j] = dot(cbt[1], ends).astype(BF16)

        @pl.when(core == 0)
        def _():
            p0(j).start()

        return carry

    lax.fori_loop(0, 4, prepare_state, 0)

    @pl.when(core == 1)
    def _():
        total(0)
        total(1)

    lane = lax.broadcasted_iota(jnp.int32, (TOK, 128), 1)
    first = lane < 64

    def intra(j, carry):
        for adjoint_at, state_at, act, part in (
            (ADJOINT_AT[0], STATE_AT[0], group_y, 0),
            (ADJOINT_AT[1], STATE_AT[1], group_x, 0),
            (ADJOINT_AT[2], STATE_AT[2], group_y, 1),
            (ADJOINT_AT[3], STATE_AT[3], group_x, 1),
            (ADJOINT_AT[4], STATE_AT[4], back_x, 0),
            (ADJOINT_AT[5], STATE_AT[5], back_x, 1),
            (ADJOINT_AT[6], STATE_AT[6], back_y, 0),
            (ADJOINT_AT[7], STATE_AT[7], back_y, 1),
        ):
            pl.when(j == core * state_at + mydir * adjoint_at)(functools.partial(act, part))
        pl.when(j < 8)(functools.partial(local, j))
        return carry

    def local(j):
        rows_l = logs[j]
        cols_l = jnp.transpose(rows_l)
        wide = columns(j)
        for way, values in ((0, g), (1, u)):
            weight = dot(wcat[way], spread[:, wide])
            wts[way, :, wide] = weight
            gi[way, :, wide] = (weight * values[:, wide].astype(F32)).astype(BF16)
        for pair in range(3):
            cols = pl.ds(pl.multiple_of(j * GROUP + pair * 128, 128), 128)
            up = u[:, cols]
            gp = g[:, cols]
            zero = jnp.zeros_like(gp)
            ys, dus = [], []
            for side in range(2):
                r = pair * 2 + side
                lr = rows_l[r : r + 1, :]
                lc = cols_l[:, r : r + 1]
                gm = jnp.where(first, gp, zero) if side == 0 else jnp.where(first, zero, gp)
                da = jnp.exp2(jnp.minimum(lc[:128] - lr[:, :128], 0.0))
                mix_a = (da * cbm[:128, :128]).astype(BF16)
                paired[:128, :128] += da * dot_nt(gm[:128], up[:128])
                db = jnp.exp2(jnp.minimum(lc[128:] - lr, 0.0))
                mix_b = (db * cbm[128:, :]).astype(BF16)
                paired[128:, :] += db * dot_nt(gm[128:], up)
                ys.append((dot(mix_a, up[:128]), dot(mix_b, up)))
                low = dot_tn(mix_b, gp[128:])
                dus.append((low[:128] + dot_tn(mix_a, gp[:128]), low[128:]))
            s0 = skip_ref[j * 6 + pair * 2]
            s1 = skip_ref[j * 6 + pair * 2 + 1]
            scale = jnp.where(first[:128], s0, s1)
            for part in range(2):
                at = slice(part * 128, part * 128 + 128)
                loc[0, at, cols] = jnp.where(first[at], ys[0][part], ys[1][part]) + scale * up[at].astype(F32)
                loc[1, at, cols] = jnp.where(first[at], dus[0][part], dus[1][part]) + scale * gp[at].astype(F32)

    lax.fori_loop(0, 9, intra, 0)

    pairs = (paired[...] * vis[...]).astype(BF16)
    acc[0] = dot(pairs, cb[1])
    acc[1] = dot_tn(pairs, cb[0])

    def carried_here(way):
        forward(0)
        for k in range(4):
            own_carry(0, k)
        forward(1)
        for k in (0, 1, 3, 2):
            own_carry(1, k)
            finish(way, came(k))

    def carried_there(way):
        for k in (0, 1, 3, 2):
            p2(0, k).wait_recv()
            p2(1, k).wait_recv()
            finish(way, at4((pos_y + k) % 4))

    @pl.when(core == 0)
    def _():
        carried_here(1)
        carried_there(0)

    @pl.when(core == 1)
    def _():
        carried_there(1)
        carried_here(0)

    proj_out[...] = acc[...].astype(BF16)

    for k in range(1, 8):
        ld_copy(k).wait_send()
        tab_copy(k).wait_send()

        @pl.when(pos_z + k < 8)
        def _():
            z1_d(k).wait_send()
            for i in range(CHUNKS):
                z1(i, k).wait_send()

    p0_d().wait_send()
    for k in range(1, 4):
        y1_d(k).wait_send()
        x1_d(k).wait_send()
    for j in range(4):
        p0(j).wait_send()
    for i in range(CHUNKS):
        for k in range(1, 4):
            for make in (y1, x1, x2, y2):
                make(i, k).wait_send()
        for k in range(4):
            p2(i, k).wait_send()


def store_kernel(values, proj, y_out, du_out, db_out, dc_out, sem):
    moves = [(proj.at[1], db_out), (proj.at[0], dc_out)]
    for part in range(4):
        rows = pl.ds(part * 64, 64)
        moves += [(values.at[0, rows], y_out.at[rows]), (values.at[1, rows], du_out.at[rows])]
    copies = [pltpu.make_async_copy(src, dst, sem.at[i]) for i, (src, dst) in enumerate(moves)]
    for one in copies:
        one.start()
    for one in copies:
        one.wait()


def body(layer_input, cotangent, b_proj, c_proj, log_decay, resets, agent_ids, skip_gain, agent_table):
    dma = pltpu.SemaphoreType.DMA
    vm = pltpu.VMEM
    any_spec = pl.BlockSpec(memory_space=pl.ANY)
    vmem_spec = pl.BlockSpec(memory_space=pltpu.VMEM)
    wide = (TOK, FEAT)
    n = CHUNKS
    hbm = [
        pltpu.with_memory_space_constraint(a, pltpu.HBM)
        for a in (
            layer_input, cotangent, b_proj, c_proj, log_decay.T, agent_table,
            resets.reshape(1, -1), agent_ids.reshape(1, -1), skip_gain,
        )
    ]
    values, proj = pl.pallas_call(
        kernel,
        out_shape=(vm((2, TOK, FEAT), BF16), vm((2, TOK, STATE), BF16)),
        in_specs=[any_spec] * 9,
        out_specs=(vmem_spec, vmem_spec),
        scratch_shapes=[
            vm(wide, BF16), vm(wide, BF16), vm((2, TOK, STATE), BF16), vm((2, STATE, TOK), BF16),
            vm((8, 8, TOK), F32), vm((8, 64, GROUP), BF16), vm((8, 8, TOK), F32),
            vm((TOK, TOK), F32), vm((TOK, TOK), F32), vm((TOK, TOK), F32),
            vm((TOK, 64), BF16), vm((2, TOK, 192), BF16), vm((192, FEAT), BF16),
            vm(wide, BF16), vm((2, TOK, FEAT), BF16), vm((2, TOK, FEAT), F32), vm((2, TOK, FEAT), F32),
            vm((2, TOK, STATE), F32),
            vm((2, 4, STATE, SLICE), BF16), vm((1, FEAT), F32), vm((4, STATE, SLICE), BF16), vm((1, FEAT), F32),
            vm((4, STATE, SLICE), BF16), vm((4, 1, SLICE), F32),
            vm((4, STATE, SLICE), BF16), vm((4, 1, SLICE), F32), vm((3, STATE, SLICE), F32),
            vm((STATE, SLICE), BF16), vm((1, SLICE), F32),
            vm((n, 4, PIECE, SLICE), BF16), vm((4, 1, SLICE), F32), vm((n, 3, PIECE, SLICE), F32),
            vm((n, PIECE, SLICE), BF16), vm((1, SLICE), F32),
            vm((n, 7, PIECE, SLICE), BF16), vm((7, 1, SLICE), F32),
            vm((n, 4, PIECE, SLICE), BF16), vm((STATE, SLICE), BF16),
            vm((4, STATE, SLICE), BF16), vm((4, STATE, SLICE), BF16), vm((2, 4, STATE, SLICE), BF16),
            dma((9,)), dma((2, 7)), dma((2, 7)), dma((4,)), dma((4,)), dma((1,)), dma((1,)),
            dma((n, 3)), dma((n, 3)), dma((3,)), dma((3,)),
            dma((n, 3)), dma((n, 3)), dma((3,)), dma((3,)),
            dma((n, 7)), dma((n, 7)), dma((7,)), dma((7,)),
            dma((n, 3)), dma((n, 3)), dma((n, 3)), dma((n, 3)), dma((n, 4)), dma((n, 4)),
            pltpu.SemaphoreType.REGULAR, vm((6, 8 * TOK), F32),
            vm((1, 8 * TOK), jnp.int32), vm((1, 8 * TOK), jnp.int32), pltpu.SMEM((48,), F32),
        ],
        compiler_params=pltpu.CompilerParams(
            collective_id=0, has_side_effects=True, vmem_limit_bytes=56 * 1024 * 1024
        ),
        name="tract_scan",
    )(*hbm)
    token = jax.ShapeDtypeStruct(wide, BF16)
    narrow = jax.ShapeDtypeStruct((TOK, STATE), BF16)
    return pl.pallas_call(
        store_kernel,
        out_shape=(token, token, narrow, narrow),
        in_specs=[any_spec] * 2,
        out_specs=(any_spec,) * 4,
        scratch_shapes=[dma((10,))],
        name="store",
    )(pltpu.with_memory_space_constraint(values, vm), pltpu.with_memory_space_constraint(proj, vm))


def solution(mesh):
    return jax.shard_map(
        body,
        mesh=mesh,
        in_specs=(
            P(("ctx", "head"), None),
            P(("ctx", "head"), None),
            P("ctx", None),
            P("ctx", None),
            P("ctx", "head"),
            P("ctx"),
            P("ctx"),
            P(),
            P(None, "head"),
        ),
        out_specs=(P(("ctx", "head"), None),) * 4,
        check_vma=False,
    )
```
